32 devices in a mesh: grp: 8 (over z, core), atm: 4 (over y, x).
Axes of the slice: x: 2, y: 2, z: 4, core: 2. Of those that a mesh axis runs over, the one named last changes fastest.
Arguments:
- atoms: float32 [2, 8192, 128], P(None, ('grp', 'atm')), may hold values from -6 to 6
- kinds: int32 [2, 8192], P(None, ('grp', 'atm')), may hold values from 0 to 3
- member: int32 [2, 8192], P(None, ('grp', 'atm')), may hold values from 0 to 7
- targets: float32 [2, 64], replicated, may hold values from -900 to 900
- weights: float32 [128, 128], replicated, may hold values from -0.5 to 0.5
- bias: float32 [128], replicated, may hold values from -0.5 to 0.5
- readout: float32 [4, 128], replicated, may hold values from -0.5 to 0.5
- covariance: float32 [16384, 16384], P('grp', 'atm'), as said below
Outputs:
- posterior: float32 [16384, 16384], P('grp', 'atm')
- weights_out: float32 [128, 128], replicated
The draws below stay inside these ranges and needn't reach their ends.
Inputs may be any that keep to these rules, and one draw needn't show every extreme that they name: `covariance`: symmetric and positive definite.
All inputs are finite; a program needn't handle non-finite values.
Results may differ from the reference program's by a relative error of at most 0.0007.
Values sent between devices are 32-bit elements; how exact they have to be, the bound alone decides.
A program may use at most 128 MiB of HBM per device.

```python
import math
import jax
import jax.numpy as jnp
from jax import lax

FEATURES = 128
PARAMS = 16384
GROUP_LOCAL = 8
GROUPS = 64
GROUP_ATOMS = 1024
ATOMS = 8192
TYPES = 4
STEPS = 2
N_GRP = 8


def draw_covariance(key, part):
    key_couple = jax.random.fold_in(key, 11)
    key_diag = jax.random.fold_in(key, 12)
    uniform_raw = jax.random.uniform(key_couple, (PARAMS, PARAMS), jnp.float32, -1.0, 1.0)
    coupling = (uniform_raw + uniform_raw.T) * (0.3 / math.sqrt(PARAMS))
    diag_values = jnp.exp(jax.random.uniform(key_diag, (PARAMS,), jnp.float32, math.log(0.8), math.log(1.6)))
    position = jnp.arange(PARAMS)
    base = coupling.at[position, position].add(diag_values)
    return base


def plant(entries, own_key, least, largest):
    dims = entries.shape
    place = [jax.random.randint(jax.random.fold_in(own_key, axis), (), 0, dims[axis]) for axis in range(len(dims))]
    entries = entries.at[tuple(place)].set(least)
    longest = dims.index(max(dims))
    place[longest] = (place[longest] + 1) % dims[longest]
    return entries.at[tuple(place)].set(largest)


def block_scale(stream_key, extent, pieces, smallest, largest):
    def one(dim, parts):
        heights = jax.random.uniform(jax.random.fold_in(jax.random.fold_in(stream_key, 6), dim), (parts,), jnp.float32, smallest / len(pieces), largest / len(pieces))
        return jnp.repeat(jnp.exp(heights), extent[dim] // parts).reshape((-1,) + (1,) * (len(extent) - dim - 1))

    level = one(*pieces[0])
    for cut in pieces[1:]:
        level = level * one(*cut)
    return level


def normal_values(stream_key, dims, spread, most, shards=(), held_as=jnp.bfloat16):
    gain = block_scale(stream_key, dims, shards, -0.22, 0.18) if shards else 1.0
    result = jax.random.normal(stream_key, dims, jnp.float32) * spread * gain
    return jnp.minimum(jnp.maximum(result, -most), most).astype(held_as)


def setup_inputs(seed: int = 0) -> dict:
    keys = jax.random.split(jax.random.key(seed), 9)
    return {
        "atoms": normal_values(keys[0], (STEPS, ATOMS, FEATURES), 1.0, 6.0, ((1, 32),), jnp.float32),
        "kinds": plant(jax.random.randint(keys[1], (STEPS, ATOMS), 0, TYPES), jax.random.fold_in(keys[1], 1), 0, TYPES - 1).astype(jnp.int32),
        "member": plant(jax.random.randint(keys[2], (STEPS, ATOMS), 0, GROUP_LOCAL), jax.random.fold_in(keys[2], 1), 0, GROUP_LOCAL - 1).astype(jnp.int32),
        "targets": normal_values(keys[3], (STEPS, GROUPS), 150.0, 900.0, (), jnp.float32),
        "weights": normal_values(keys[4], (FEATURES, FEATURES), FEATURES ** -0.5, 0.5, (), jnp.float32),
        "bias": jnp.clip(jax.random.uniform(keys[5], (FEATURES,), jnp.float32, -0.5, 0.5), -0.5, 0.5),
        "readout": normal_values(keys[6], (TYPES, FEATURES), FEATURES ** -0.5, 0.5, (), jnp.float32),
        "covariance": draw_covariance(jax.random.fold_in(keys[8], 71), 0),
    }


forget_rate = 0.98

def local_terms(atoms, kinds, member, weights, bias, readout):
    precise = lax.Precision.HIGHEST
    preact = jnp.dot(atoms.astype(jnp.float32), weights.astype(jnp.float32), precision=precise, preferred_element_type=jnp.float32) + bias
    hidden = jnp.tanh(preact)
    type_hot = (kinds[:, None] == jnp.arange(readout.shape[0])[None, :]).astype(jnp.float32)
    vectors = jnp.dot(type_hot, readout, precision=precise)
    atom_energy = jnp.sum(hidden * vectors, axis=1)
    slope = (1.0 - hidden * hidden) * vectors
    group_hot = (member[:, None] == jnp.arange(GROUP_LOCAL)[None, :]).astype(jnp.float32)
    energies = jnp.dot(atom_energy, group_hot, precision=precise)
    masked = atoms[:, None, :] * group_hot[:, :, None]
    grads = jnp.einsum('agi,ac->gic', masked, slope, precision=precise)
    return (energies, grads.reshape(GROUP_LOCAL, FEATURES * FEATURES))

def reference(atoms, kinds, member, targets, weights, bias, readout, covariance):
    precise = lax.Precision.HIGHEST
    current = weights
    covar = covariance
    identity = jnp.eye(GROUPS, dtype=jnp.float32)
    for update_idx in range(STEPS):

        def block_terms(inputs, current=current):
            return local_terms(inputs[0], inputs[1], inputs[2], current, bias, readout)
        energies, grads = lax.map(block_terms, (atoms[update_idx].reshape(N_GRP, GROUP_ATOMS, FEATURES), kinds[update_idx].reshape(N_GRP, GROUP_ATOMS), member[update_idx].reshape(N_GRP, GROUP_ATOMS)))
        predicted = energies.reshape(GROUPS)
        jacobian = grads.reshape(GROUPS, PARAMS)
        mismatch = targets[update_idx] - predicted
        gains = jnp.dot(covar, jacobian.T, precision=precise)
        curvature = jnp.dot(jacobian, gains, precision=precise)
        innovation = 0.5 * (curvature + curvature.T) + forget_rate * identity
        factor = jnp.linalg.cholesky(innovation)
        inverse = jax.scipy.linalg.cho_solve((factor, True), identity)
        coefficient = jnp.dot(inverse, mismatch, precision=precise)
        change = jnp.dot(gains, coefficient, precision=precise)
        current = current + change.reshape(FEATURES, FEATURES)
        scaled = jnp.dot(gains, inverse, precision=precise)
        covar = (covar - jnp.dot(scaled, gains.T, precision=precise)) / forget_rate
    return (covar, current)
```

```python
import functools
import jax
import jax.numpy as jnp
from jax import lax
from jax.experimental import pallas as pl
from jax.experimental.pallas import tpu as pltpu
from jax.sharding import PartitionSpec as P

GROUP_LOCAL = 8
STEPS = 2
CORES = 2
LANES = 128
CHUNKS = 2

forget_rate = 0.98
precise = lax.Precision.HIGHEST
MESH = pl.DeviceIdType.MESH
VM = pl.BlockSpec(memory_space=pltpu.VMEM)


def local_terms(atoms, kinds, member, weights, bias, readout):
    preact = jnp.dot(atoms, weights, precision=precise, preferred_element_type=jnp.float32) + bias
    hidden = jnp.tanh(preact)
    type_hot = (kinds[:, None] == jnp.arange(readout.shape[0])[None, :]).astype(jnp.float32)
    vectors = jnp.dot(type_hot, readout, precision=precise)
    atom_energy = jnp.sum(hidden * vectors, axis=1)
    slope = (1.0 - hidden * hidden) * vectors
    group_hot = (member[:, None] == jnp.arange(GROUP_LOCAL)[None, :]).astype(jnp.float32)
    energies = jnp.dot(atom_energy, group_hot, precision=precise)
    masked = atoms[:, None, :] * group_hot[:, :, None]
    grads = jnp.einsum("agi,ac->gic", masked, slope, precision=precise)
    return energies, grads.reshape(GROUP_LOCAL, -1)


def push(src, dst, sems, recvs, slot, target):
    copy = pltpu.make_async_remote_copy(
        src_ref=src, dst_ref=dst, send_sem=sems.at[slot], recv_sem=recvs.at[slot],
        device_id=target, device_id_type=MESH,
    )
    copy.start()
    return copy


def greet(targets):
    barrier = pltpu.get_barrier_semaphore()
    for target in targets:
        pl.semaphore_signal(barrier, inc=1, device_id=target, device_id_type=MESH)
    pl.semaphore_wait(barrier, len(targets))


def places(n_grp, n_atm):
    row, col = lax.axis_index("grp"), lax.axis_index("atm")
    n_z = n_grp // CORES
    z, core = row // CORES, lax.rem(row, CORES)
    plane = [lax.rem(col + d, n_atm) for d in range(1, n_atm)]
    column = [lax.rem(z + d, n_z) * CORES + core for d in range(1, n_z)]
    partner = z * CORES + (CORES - 1 - core)
    return row, col, z, core, plane, column, partner


def grads_kernel(n_grp, n_atm, x_ref, out_ref, got, a_s, a_r, b_s, b_r, f_s, f_r):
    row, col, z, core, plane, column, partner = places(n_grp, n_atm)
    greet([{"atm": p} for p in plane] + [{"grp": p} for p in column] + [{"grp": partner}])
    n_z = n_grp // CORES
    wide = x_ref.shape[2]
    middle = wide // 2 // LANES * LANES
    cuts = [pl.ds(0, middle), pl.ds(middle, wide - middle)]
    first, second, last = [], [], []
    for k, cut in enumerate(cuts):
        first.append([push(x_ref.at[p, :, cut], got.at[i, :, cut], a_s.at[k], a_r.at[k], i, {"atm": p}) for i, p in enumerate(plane)])
    for k, cut in enumerate(cuts):
        total = x_ref[col, :, cut]
        for i, copy in enumerate(first[k]):
            copy.wait_recv()
            total = total + got[i, :, cut]
        out_ref[row, :, cut] = total
        place = out_ref.at[row, :, cut]
        second.append([push(place, place, b_s.at[k], b_r.at[k], i, {"grp": p}) for i, p in enumerate(column)])
        last.append(push(place, place, f_s.at[k], f_r.at[k], len(column), {"grp": partner}))
    for k, cut in enumerate(cuts):
        for i, copy in enumerate(second[k]):
            copy.wait_recv()
            origin = lax.rem(z + n_z - (i + 1), n_z) * CORES + core
            place = out_ref.at[origin, :, cut]
            last.append(push(place, place, f_s.at[k], f_r.at[k], i, {"grp": partner}))
    for copy in last:
        copy.wait_recv()
    for copy in sum(first + second, last):
        copy.wait_send()


def share_grads(x, n_grp, n_atm):
    block = x.shape[1:]
    n_z = n_grp // CORES
    dma = pltpu.SemaphoreType.DMA
    return pl.pallas_call(
        functools.partial(grads_kernel, n_grp, n_atm),
        out_shape=jax.ShapeDtypeStruct((n_grp,) + block, jnp.float32),
        in_specs=[VM], out_specs=VM,
        scratch_shapes=[pltpu.VMEM((n_atm - 1,) + block, jnp.float32)]
        + [dma((2, n_atm - 1))] * 2 + [dma((2, n_z - 1))] * 2 + [dma((2, n_z))] * 2,
        compiler_params=pltpu.CompilerParams(collective_id=0, has_side_effects=True),
        name="share_grads",
    )(x)


def gains_kernel(n_grp, n_atm, half, t_ref, row_ref, col_ref, got, quarter,
                 a_s, a_r, r_s, r_r, b_s, b_r, c_s, c_r, f_s, f_r):
    row, col, z, core, plane, column, partner = places(n_grp, n_atm)
    greet([{"atm": p} for p in plane] + [{"grp": p} for p in column] + [{"grp": partner}])
    groups = t_ref.shape[1]
    chunk = groups // CHUNKS
    cuts = [pl.ds(k * chunk, chunk) for k in range(CHUNKS)]
    first, along, rows, across, last = [], [], [], [], []
    for k, cut in enumerate(cuts):
        first.append([push(t_ref.at[p, cut], got.at[i, cut], a_s.at[k], a_r.at[k], i, {"atm": p}) for i, p in enumerate(plane)])
    for k, cut in enumerate(cuts):
        total = t_ref[col, cut]
        for i, copy in enumerate(first[k]):
            copy.wait_recv()
            total = total + got[i, cut]
        quarter[z, cut] = total
        row_ref[col, cut] = total
        along.append([push(quarter.at[z, cut], quarter.at[z, cut], b_s.at[k], b_r.at[k], i, {"grp": p}) for i, p in enumerate(column)])
        rows.append([push(row_ref.at[col, cut], row_ref.at[col, cut], r_s.at[k], r_r.at[k], i, {"atm": p}) for i, p in enumerate(plane)])
    for k, cut in enumerate(cuts):
        for copy in along[k]:
            copy.wait_recv()
        across.append([
            push(quarter.at[pl.ds(p * half, half), cut], col_ref.at[core, col, :, cut], c_s.at[k], c_r.at[k], i, {"atm": p})
            for i, p in enumerate(plane)
        ])
        col_ref[core, col, :, cut] = quarter[pl.ds(col * half, half), cut]
        place = col_ref.at[core, col, :, cut]
        last.append([push(place, place, f_s.at[k], f_r.at[k], len(plane), {"grp": partner})])
    for k, cut in enumerate(cuts):
        for i, copy in enumerate(across[k]):
            copy.wait_recv()
            origin = lax.rem(col + n_atm - (i + 1), n_atm)
            place = col_ref.at[core, origin, :, cut]
            last[k].append(push(place, place, f_s.at[k], f_r.at[k], i, {"grp": partner}))
    for group in rows + last:
        for copy in group:
            copy.wait_recv()
    for group in first + along + rows + across + last:
        for copy in group:
            copy.wait_send()


def share_gains(t, n_grp, n_atm):
    _, groups, piece = t.shape
    per_col = n_grp // n_atm
    if n_grp % n_atm or per_col % CORES:
        mine = lax.psum(t, "atm")
        full = lax.all_gather(mine, "grp", axis=0).transpose(2, 0, 1, 3).reshape(groups, -1)
        width = full.shape[1] // n_atm
        return mine, lax.dynamic_slice_in_dim(full, lax.axis_index("atm") * width, width, 1)
    half = per_col // CORES
    n_z = n_grp // CORES
    dma = pltpu.SemaphoreType.DMA
    vm = lambda *lead: pltpu.VMEM(lead + (groups, piece), jnp.float32)
    rows, cols = pl.pallas_call(
        functools.partial(gains_kernel, n_grp, n_atm, half),
        out_shape=(
            jax.ShapeDtypeStruct((n_atm, groups, piece), jnp.float32),
            jax.ShapeDtypeStruct((CORES, n_atm, half, groups, piece), jnp.float32),
        ),
        in_specs=[VM], out_specs=(VM, VM),
        scratch_shapes=[vm(n_atm - 1), vm(n_z)]
        + [dma((CHUNKS, n_atm - 1))] * 4 + [dma((CHUNKS, n_z - 1))] * 2 + [dma((CHUNKS, n_atm - 1))] * 2 + [dma((CHUNKS, n_atm))] * 2,
        compiler_params=pltpu.CompilerParams(collective_id=1, has_side_effects=True),
        name="share_gains",
    )(t)
    return rows, cols.transpose(3, 2, 0, 1, 4).reshape(groups, -1)


def gather_kernel(n_atm, v_ref, out_ref, s, r):
    col = lax.axis_index("atm")
    plane = [lax.rem(col + d, n_atm) for d in range(1, n_atm)]
    greet([{"atm": p} for p in plane])
    copies = [push(v_ref, out_ref.at[col], s, r, i, {"atm": p}) for i, p in enumerate(plane)]
    out_ref[col] = v_ref[...]
    for copy in copies:
        copy.wait()


def gather_atm(v, n_atm, ident):
    return pl.pallas_call(
        functools.partial(gather_kernel, n_atm),
        out_shape=jax.ShapeDtypeStruct((n_atm,) + v.shape, jnp.float32),
        in_specs=[VM], out_specs=VM,
        scratch_shapes=[pltpu.SemaphoreType.DMA((n_atm - 1,))] * 2,
        compiler_params=pltpu.CompilerParams(collective_id=ident, has_side_effects=True),
        name="gather_atm%d" % ident,
    )(v)


def inverse_kernel(parts_ref, out_ref, work):
    size = out_ref.shape[0]
    total = parts_ref[0]
    for k in range(1, parts_ref.shape[0]):
        total = total + parts_ref[k]
    down = lax.broadcasted_iota(jnp.int32, (size, size), 0)
    over = lax.broadcasted_iota(jnp.int32, (size, size), 1)
    work[...] = 0.5 * (total + total.T) + jnp.where(down == over, forget_rate, 0.0)

    def sweep(k, carry):
        full = work[...]
        row = work[pl.ds(k, 1), :]
        column = jnp.sum(jnp.where(over == k, full, 0.0), axis=1, keepdims=True)
        pivot = 1.0 / jnp.sum(jnp.where(over[:1] == k, row, 0.0), axis=1, keepdims=True)
        row_part, col_part = row * pivot, column * pivot
        swept = full - column * row_part
        swept = jnp.where(down == k, row_part, swept)
        swept = jnp.where(over == k, col_part, swept)
        work[...] = jnp.where((down == k) & (over == k), -pivot, swept)
        return carry

    lax.fori_loop(0, size, sweep, 0)
    out_ref[...] = -work[...]


def innovation_inverse(parts):
    size = parts.shape[-1]
    return pl.pallas_call(
        inverse_kernel,
        out_shape=jax.ShapeDtypeStruct((size, size), jnp.float32),
        in_specs=[VM], out_specs=VM,
        scratch_shapes=[pltpu.VMEM((size, size), jnp.float32)],
        name="innovation_inverse",
    )(parts)


def split(value):
    high = value.astype(jnp.bfloat16)
    return high, (value - high.astype(jnp.float32)).astype(jnp.bfloat16)


def across(a, b, **options):
    return lax.dot_general(a, b, (((1,), (1,)), ((), ())), preferred_element_type=jnp.float32, **options)


def spd_inverse(value):
    size = value.shape[0]
    down = lax.broadcasted_iota(jnp.int32, (size, size), 0)
    over = lax.broadcasted_iota(jnp.int32, (size, size), 1)
    for k in range(size):
        column, row = value[:, k:k + 1], value[k:k + 1, :]
        pivot = 1.0 / value[k:k + 1, k:k + 1]
        scaled = jnp.where(over[:1] == k, 1.0, row) * pivot
        rest = jnp.where(over == k, 0.0, value) - column * scaled
        value = jnp.where(down == k, scaled, rest)
    return value


def fused_kernel(n_grp, n_atm, *refs):
    (atoms_ref, kinds_ref, member_ref, targets_ref, weights_ref, bias_ref, readout_ref, p_hbm,
     p_ref, rows0, cols0, rows1, cols1, mats_ref, w_ref,
     xt_ref, jpart, jgot, jall, both, tacc, tpart, tgot, jpiece, gpiece, quarter, cplane, cz, wplane, wz,
     p_sem, j_s, j_r, z_s, z_r, f_s, f_r, i_s, i_r, t_s, t_r, c_s, c_r, d_s, d_r, w_s, w_r, v_s, v_r,
     gr_s, gr_r, gz_s, gz_r, ga_s, ga_r, gf_s, gf_r) = refs
    rows_out, cols_out = (rows0, rows1), (cols0, cols1)
    row, col, z, core, plane, column, partner = places(n_grp, n_atm)
    n_z = n_grp // CORES
    seat = core * n_atm + col
    seats = CORES * n_atm
    others = [lax.rem(seat + d, seats) for d in range(1, seats)]
    floor = [{"grp": z * CORES + o // n_atm, "atm": lax.rem(o, n_atm)} for o in others]
    groups = GROUP_LOCAL * n_grp
    rows, width = p_ref.shape
    features = weights_ref.shape[0]
    units = weights_ref.shape[1]
    local = jpart.shape[2] - 1
    chunk = local // CHUNKS
    span = chunk * units
    piece = rows // n_atm
    per = piece // units
    tile = min(piece, 256)

    loads = []
    for k in range(CHUNKS):
        cut = pl.ds(k * span, span)
        load = pltpu.make_async_copy(p_hbm.at[:, cut], p_ref.at[:, cut], p_sem.at[k])
        load.start()
        loads.append(load)

    for step in range(STEPS):
        xt_ref[step] = atoms_ref[step].T
    greet(floor + [{"grp": p} for p in column])

    current = weights_ref[...]
    inverses, sends, bulk = [], [], {}
    iota8 = lax.broadcasted_iota(jnp.int32, (GROUP_LOCAL, units), 0)

    def gains_first(step):
        here = gpiece[step]
        rows_out[step][col] = here
        quarter[step, z] = here
        far = [push(quarter.at[step, z], quarter.at[step, z], gz_s.at[step], gz_r.at[step], i, {"grp": p}) for i, p in enumerate(column)]
        near = [push(rows_out[step].at[col], rows_out[step].at[col], gr_s.at[step], gr_r.at[step], i, {"atm": p}) for i, p in enumerate(plane)]
        bulk[step] = [far, near]

    def gains_second(step):
        for copy in bulk[step][0]:
            copy.wait_recv()
        out = cols_out[step]
        swap = [push(quarter.at[step, p], out.at[core, col], ga_s.at[step], ga_r.at[step], i, {"atm": p}) for i, p in enumerate(plane)]
        out[core, col] = quarter[step, col]
        place = out.at[core, col]
        last = [push(place, place, gf_s.at[step], gf_r.at[step], len(plane), {"grp": partner})]
        bulk[step] += [swap, last]

    def gains_third(step):
        out = cols_out[step]
        for i, copy in enumerate(bulk[step][2]):
            copy.wait_recv()
            origin = lax.rem(col + n_atm - (i + 1), n_atm)
            place = out.at[core, origin]
            bulk[step][3].append(push(place, place, gf_s.at[step], gf_r.at[step], i, {"grp": partner}))

    def gains_last(step):
        far, near, swap, last = bulk[step]
        for copy in near + last:
            copy.wait_recv()
        for copy in far + near + swap + last:
            copy.wait_send()

    for step in range(STEPS):
        x = atoms_ref[step]
        preact = jnp.dot(x, current, precision=precise, preferred_element_type=jnp.float32) + bias_ref[...]
        hidden = jnp.tanh(preact)
        kinds_row = kinds_ref[step:step + 1, :].astype(jnp.float32)
        kinds_col = jnp.broadcast_to(kinds_row, (GROUP_LOCAL, kinds_row.shape[1])).T[:, :1]
        vectors = jnp.zeros_like(hidden)
        for kind in range(readout_ref.shape[0]):
            vectors = jnp.where(kinds_col == kind, readout_ref[kind:kind + 1, :], vectors)
        slope = (1.0 - hidden * hidden) * vectors
        slope_high, slope_low = split(slope)
        slope_both = jnp.concatenate([slope_high, slope_low], axis=1)
        n_own = x.shape[0]
        member_row = member_ref[step:step + 1, :]
        hot = (lax.broadcasted_iota(jnp.int32, (GROUP_LOCAL, n_own), 0) == member_row).astype(jnp.float32)
        energy = jnp.dot(hot, hidden * vectors, precision=precise, preferred_element_type=jnp.float32)
        energy = jnp.broadcast_to(jnp.sum(energy, axis=1, keepdims=True), (GROUP_LOCAL, units))

        def grads(p):
            xs = xt_ref[step, pl.ds(p * local, local), :]
            high = xs.astype(jnp.bfloat16).astype(jnp.float32)
            pick = lambda v: (v[:, None, :] * hot[None]).reshape(local * GROUP_LOCAL, n_own).astype(jnp.bfloat16)
            one = jnp.dot(pick(high), slope_both, preferred_element_type=jnp.float32)
            two = jnp.dot(pick(xs - high), slope_high, preferred_element_type=jnp.float32)
            total = one[:, :units] + one[:, units:] + two
            jpart[step, p, :local] = total.reshape(local, GROUP_LOCAL, units)
            jpart[step, p, local] = energy

        for p in plane:
            grads(p)
        cuts = [pl.ds(k * chunk, chunk + (1 if k == CHUNKS - 1 else 0)) for k in range(CHUNKS)]
        first = [[push(jpart.at[step, p, cut], jgot.at[step, i, cut], j_s.at[step, k], j_r.at[step, k], i, {"atm": p})
                  for i, p in enumerate(plane)] for k, cut in enumerate(cuts)]
        grads(col)
        second, third = [], []
        for k, cut in enumerate(cuts):
            total = jpart[step, col, cut]
            for i, copy in enumerate(first[k]):
                copy.wait_recv()
                total = total + jgot[step, i, cut]
            jall[step, row, cut] = total
            place = jall.at[step, row, cut]
            second.append([push(place, place, z_s.at[step, k], z_r.at[step, k], i, {"grp": p}) for i, p in enumerate(column)])
            third.append([push(place, place, f_s.at[step, k], f_r.at[step, k], len(column), {"grp": partner})])
        sends += sum(first + second, [])

        def product(at, k):
            high, low = split(p_ref[pl.ds(at, tile), k * span:(k + 1) * span])
            right = both[step, :, k * span:(k + 1) * span]
            return across(high, right) + across(low, right)

        scatter = []
        for k, cut in enumerate(cuts):
            for i, copy in enumerate(second[k]):
                copy.wait_recv()
                origin = lax.rem(z + n_z - (i + 1), n_z) * CORES + core
                place = jall.at[step, origin, cut]
                third[k].append(push(place, place, f_s.at[step, k], f_r.at[step, k], i, {"grp": partner}))
            for copy in third[k]:
                copy.wait_recv()
            sends += third[k]
            for i in range(k * chunk, (k + 1) * chunk):
                high, low = split(jall[step, :, i].reshape(groups, units))
                both[step, :groups, i * units:(i + 1) * units] = high
                both[step, groups:, i * units:(i + 1) * units] = low
            if step == 0:
                loads[k].wait()
            if k < CHUNKS - 1:
                def body_tile(t, carry):
                    at = pl.multiple_of(t * tile, tile)
                    value = product(at, k)
                    tacc[pl.ds(at, tile), :] = value if k == 0 else tacc[pl.ds(at, tile), :] + value
                    return carry
                lax.fori_loop(0, rows // tile, body_tile, 0)
            else:
                inner = local // CORES
                window = lambda p: pl.ds(core * inner + p * per, per)
                jp_copies = [pltpu.make_async_remote_copy(
                    src_ref=jall.at[step, :, window(p)], dst_ref=jpiece.at[step], send_sem=i_s.at[step, i], recv_sem=i_r.at[step],
                    device_id={"atm": p}, device_id_type=MESH) for i, p in enumerate(plane)]

                @pl.when(col == z)
                def _():
                    for copy in jp_copies:
                        copy.start()
                    jpiece[step] = jall[step, :, window(col)]

                for i, p in enumerate(plane + [col]):
                    def last_tile(t, carry):
                        at = pl.multiple_of(p * piece + t * tile, tile)
                        value = product(at, k)
                        if k > 0:
                            value = value + tacc[pl.ds(at, tile), :]
                        value = value.T
                        tpart[step, p, :, pl.ds(pl.multiple_of(t * tile, tile), tile)] = value[:groups] + value[groups:]
                        return carry
                    lax.fori_loop(0, piece // tile, last_tile, 0)
                    if i < len(plane):
                        scatter.append(push(tpart.at[step, p], tgot.at[step, i], t_s.at[step], t_r.at[step], i, {"atm": p}))
        sends += scatter
        gain = tpart[step, col]
        for i, copy in enumerate(scatter):
            copy.wait_recv()
            gain = gain + tgot[step, i]
        gpiece[step] = gain
        if step == STEPS - 1:
            gains_first(step)

        @pl.when(col != z)
        def _():
            jp_copies[0].wait_recv()

        @pl.when(col == z)
        def _():
            for copy in jp_copies:
                copy.wait_send()

        jp = jnp.concatenate([jpiece[step, :, j].reshape(groups, units) for j in range(per)], axis=1)
        stack = gain if step == 0 else jnp.concatenate([gain] + [gpiece[s] for s in range(step)], axis=0)
        terms = across(jp, stack, precision=precise)
        if step == 0:
            terms = jnp.concatenate([terms[:groups // 2], terms[groups // 2:]], axis=1)
        size = pl.ds(0, terms.shape[0])
        cplane[step, seat, size] = terms
        hop = [push(cplane.at[step, seat, size], cplane.at[step, seat, size], c_s.at[step], c_r.at[step], i, d) for i, d in enumerate(floor)]
        for copy in hop:
            copy.wait_recv()
        terms = cplane[step, 0, size]
        for i in range(1, seats):
            terms = terms + cplane[step, i, size]
        cz[step, z, size] = terms
        skip = [push(cz.at[step, z, size], cz.at[step, z, size], d_s.at[step], d_r.at[step], i, {"grp": p}) for i, p in enumerate(column)]
        for copy in skip:
            copy.wait_recv()
        sends += hop + skip
        terms = cz[step, 0, size]
        for i in range(1, n_z):
            terms = terms + cz[step, i, size]
        if step < STEPS - 1:
            gains_first(step)

        if step == 0:
            curve = jnp.concatenate([terms[:, :groups], terms[:, groups:]], axis=0)
        else:
            cross = terms[:, groups:]
            early = jnp.dot(cross, inverses[0], precision=precise, preferred_element_type=jnp.float32)
            curve = (terms[:, :groups] - across(early, cross, precision=precise)) * (1.0 / forget_rate)
        down = lax.broadcasted_iota(jnp.int32, (groups, groups), 0)
        over = lax.broadcasted_iota(jnp.int32, (groups, groups), 1)
        inverse = spd_inverse(0.5 * (curve + curve.T) + jnp.where(down == over, forget_rate, 0.0))
        inverses.append(inverse)
        mats_ref[step] = inverse * (1.0 / forget_rate ** (STEPS - step))
        if step > 0:
            mats_ref[STEPS] = early
            gain = gain - jnp.dot(early, gpiece[0], precision=precise, preferred_element_type=jnp.float32)
            gain = gain * (1.0 / forget_rate)
            gains_second(step)

        predicted = jall[step, :, local].reshape(groups, units).T
        mismatch = jnp.broadcast_to(targets_ref[step:step + 1, :], (GROUP_LOCAL, groups)) - predicted[:GROUP_LOCAL]
        coefficient = jnp.dot(mismatch, inverse, precision=precise, preferred_element_type=jnp.float32)
        change = jnp.dot(coefficient, gain, precision=precise, preferred_element_type=jnp.float32)
        turn = lax.rem(iota8, per)
        mine = change[:, :units]
        for j in range(1, per):
            mine = jnp.where(turn == j, change[:, j * units:(j + 1) * units], mine)
        wplane[step, seat] = mine
        hop = [push(wplane.at[step, seat], wplane.at[step, seat], w_s.at[step], w_r.at[step], i, d) for i, d in enumerate(floor)]
        for copy in hop:
            copy.wait_recv()
        fold = GROUP_LOCAL // per
        for m in range(seats // fold):
            dense = wplane[step, m * fold]
            for j in range(1, fold):
                dense = jnp.where(iota8 >= j * per, wplane[step, m * fold + j], dense)
            wz[step, z, m * GROUP_LOCAL:(m + 1) * GROUP_LOCAL] = dense
        skip = [push(wz.at[step, z], wz.at[step, z], v_s.at[step], v_r.at[step], i, {"grp": p}) for i, p in enumerate(column)]
        if step == 0:
            gains_second(step)
        for copy in skip:
            copy.wait_recv()
        sends += hop + skip
        current = current + wz[step].reshape(features, units)
        gains_third(step)

    w_ref[...] = current
    for step in range(STEPS):
        gains_last(step)
    for copy in sends:
        copy.wait_send()


def fused(atoms, kinds, member, targets, weights, bias, readout, covariance, n_grp, n_atm):
    rows, width = covariance.shape
    units = weights.shape[1]
    groups = GROUP_LOCAL * n_grp
    n_z = n_grp // CORES
    seats = CORES * n_atm
    local = width // units
    piece = rows // n_atm
    per = piece // units
    block = (local + 1, GROUP_LOCAL, units)
    f32 = jnp.float32
    dma = pltpu.SemaphoreType.DMA
    vm = lambda *shape: pltpu.VMEM(shape, f32)
    pair = lambda *shape: [dma((STEPS,) + shape)] * 2
    out_shape = (
        vm(rows, width),
        vm(n_atm, groups, piece), vm(CORES, n_atm, groups, piece),
        vm(n_atm, groups, piece), vm(CORES, n_atm, groups, piece),
        vm(STEPS + 1, groups, groups), vm(*weights.shape),
    )
    outs = pl.pallas_call(
        functools.partial(fused_kernel, n_grp, n_atm),
        out_shape=out_shape,
        in_specs=[VM] * 7 + [pl.BlockSpec(memory_space=pltpu.HBM)],
        out_specs=(VM,) * len(out_shape),
        scratch_shapes=[
            vm(STEPS, atoms.shape[2], atoms.shape[1]),
            vm(STEPS, n_atm, *block), vm(STEPS, n_atm - 1, *block), vm(STEPS, n_grp, *block),
            pltpu.VMEM((STEPS, 2 * groups, width), jnp.bfloat16),
            vm(rows, 2 * groups),
            vm(STEPS, n_atm, groups, piece), vm(STEPS, n_atm - 1, groups, piece),
            vm(STEPS, n_grp, per, GROUP_LOCAL, units), vm(STEPS, groups, piece), vm(STEPS, n_z, groups, piece),
            vm(STEPS, seats, groups, STEPS * groups), vm(STEPS, n_z, groups, STEPS * groups),
            vm(STEPS, seats, GROUP_LOCAL, units), vm(STEPS, n_z, seats * per, units),
            dma((CHUNKS,)),
        ] + pair(CHUNKS, n_atm - 1) + pair(CHUNKS, n_z - 1) + pair(CHUNKS, n_z)
        + [dma((STEPS, n_atm - 1)), dma((STEPS,))] + pair(n_atm - 1)
        + pair(seats - 1) + pair(n_z - 1) + pair(seats - 1) + pair(n_z - 1)
        + pair(n_atm - 1) + pair(n_z - 1) + pair(n_atm - 1) + pair(n_atm),
        compiler_params=pltpu.CompilerParams(collective_id=4, has_side_effects=True, vmem_limit_bytes=24 << 20),
        name="updates",
    )(atoms, kinds, member, targets, weights, bias.reshape(1, -1), readout, covariance)
    return [pltpu.with_memory_space_constraint(out, pltpu.VMEM) for out in outs]


def triple(a, b):
    high, low = split(a)
    high_b, low_b = split(b)
    left = jnp.concatenate([high, low, high], axis=1)
    right = jnp.concatenate([high_b, high_b, low_b], axis=0)
    return jnp.dot(left, right, preferred_element_type=jnp.float32)


def finish_kernel(tile, p_ref, rows0, cols0, rows1, cols1, mats_ref, w_in, out_ref, w_out, left, right):
    groups = mats_ref.shape[1]
    n_atm = rows0.shape[0]
    piece = rows0.shape[2]

    @pl.when(pl.program_id(0) == 0)
    def _():
        w_out[...] = w_in[...]
        both = jnp.concatenate([mats_ref[0], mats_ref[2]], axis=0)
        for b in range(CORES * n_atm):
            one = triple(both, cols0[b // n_atm, b % n_atm])
            later = (cols1[b // n_atm, b % n_atm] - one[groups:]) * (1.0 / forget_rate)
            high, low = split(jnp.concatenate([one[:groups], triple(mats_ref[1], later)], axis=0))
            cut = slice(b * piece, (b + 1) * piece)
            right[:, cut] = jnp.concatenate([high, high, low], axis=0)
        for p in range(n_atm):
            later = (rows1[p] - triple(mats_ref[2], rows0[p])) * (1.0 / forget_rate)
            high, low = split(jnp.concatenate([rows0[p], later], axis=0).T)
            left[p * piece:(p + 1) * piece, :] = jnp.concatenate([high, low, high], axis=1)

    here = pl.ds(pl.multiple_of(pl.program_id(0) * tile, tile), tile)
    width = out_ref.shape[1]
    part = min(width, 512)
    for k in range(0, width, part):
        down = jnp.dot(left[here, :], right[:, k:k + part], preferred_element_type=jnp.float32)
        out_ref[:, k:k + part] = p_ref[here, k:k + part] * (1.0 / forget_rate ** STEPS) - down


def finish(covar, rows0, cols0, rows1, cols1, mats, weights):
    rows, width = covar.shape
    groups = mats.shape[1]
    tile = min(rows, 128)
    return pl.pallas_call(
        functools.partial(finish_kernel, tile),
        grid=(rows // tile,),
        out_shape=(jax.ShapeDtypeStruct((rows, width), jnp.float32), jax.ShapeDtypeStruct(weights.shape, jnp.float32)),
        in_specs=[VM] * 7,
        out_specs=(pl.BlockSpec((tile, width), lambda i: (i, 0)), pl.BlockSpec(weights.shape, lambda i: (0, 0))),
        scratch_shapes=[
            pltpu.VMEM((rows, 3 * STEPS * groups), jnp.bfloat16),
            pltpu.VMEM((3 * STEPS * groups, width), jnp.bfloat16),
        ],
        compiler_params=pltpu.CompilerParams(vmem_limit_bytes=22 << 20),
        name="finish",
    )(covar, rows0, cols0, rows1, cols1, mats, weights)


def terms_kernel(groups, jac_ref, p_ref, out_ref, both):
    @pl.when(pl.program_id(0) == 0)
    def _():
        jac = jac_ref[...]
        high = jac.astype(jnp.bfloat16).astype(jnp.float32)
        both[...] = jnp.concatenate([high, jac - high], axis=0).T.astype(jnp.bfloat16)

    high, low = split(p_ref[...])
    one = jnp.dot(high, both[...], preferred_element_type=jnp.float32)
    two = jnp.dot(low, both[...], preferred_element_type=jnp.float32)
    one = one.T
    out_ref[0] = one[:groups] + one[groups:] + two.T[:groups]


def row_terms(covar, jac, n_atm):
    rows, width = covar.shape
    groups = jac.shape[0]
    piece = rows // n_atm
    tile = min(piece, 256)
    per = piece // tile
    return pl.pallas_call(
        functools.partial(terms_kernel, groups),
        grid=(rows // tile,),
        out_shape=jax.ShapeDtypeStruct((n_atm, groups, piece), jnp.float32),
        in_specs=[
            pl.BlockSpec((groups, width), lambda i: (0, 0)),
            pl.BlockSpec((tile, width), lambda i: (i, 0)),
        ],
        out_specs=pl.BlockSpec((1, groups, tile), lambda i: (i // per, 0, lax.rem(i, per))),
        scratch_shapes=[pltpu.VMEM((width, 2 * groups), jnp.bfloat16)],
        compiler_params=pltpu.CompilerParams(vmem_limit_bytes=48 << 20),
        name="row_terms",
    )(jac, covar)


def update_kernel(scale, left_ref, right_ref, p_ref, out_ref, right):
    @pl.when(pl.program_id(0) == 0)
    def _():
        high, low = split(right_ref[...])
        right[...] = jnp.concatenate([high, high, low], axis=0)

    high, low = split(left_ref[...])
    left = jnp.concatenate([high, low, high], axis=1)
    width = p_ref.shape[1]
    part = min(width, 512)
    for k in range(0, width, part):
        down = jnp.dot(left, right[:, k:k + part], preferred_element_type=jnp.float32)
        out_ref[:, k:k + part] = p_ref[:, k:k + part] * scale - down


def final_update(covar, left, right):
    rows, width = covar.shape
    depth = left.shape[1]
    tile = min(rows, 256)
    return pl.pallas_call(
        functools.partial(update_kernel, 1.0 / forget_rate ** STEPS),
        grid=(rows // tile,),
        out_shape=jax.ShapeDtypeStruct((rows, width), jnp.float32),
        in_specs=[
            pl.BlockSpec((tile, depth), lambda i: (i, 0)),
            pl.BlockSpec((depth, width), lambda i: (0, 0)),
            pl.BlockSpec((tile, width), lambda i: (i, 0)),
        ],
        out_specs=pl.BlockSpec((tile, width), lambda i: (i, 0)),
        scratch_shapes=[pltpu.VMEM((3 * depth, width), jnp.bfloat16)],
        compiler_params=pltpu.CompilerParams(vmem_limit_bytes=48 << 20),
        name="final_update",
    )(left, right, covar)


def body(atoms, kinds, member, targets, weights, bias, readout, covariance):
    n_grp, n_atm = lax.axis_size("grp"), lax.axis_size("atm")
    rows, width = covariance.shape
    units = weights.shape[1]
    if n_grp == CORES * n_atm and rows % (n_atm * units) == 0 and units % LANES == 0 and GROUP_LOCAL % (rows // (n_atm * units)) == 0:
        covar, *gains, mats, current = fused(atoms, kinds, member, targets, weights, bias, readout, covariance, n_grp, n_atm)
        return finish(covar, *gains, mats, current)
    groups = GROUP_LOCAL * n_grp
    dot = functools.partial(jnp.dot, precision=precise)
    current = weights
    past = []
    for step in range(STEPS):
        energies, partial_value = local_terms(
            atoms[step], kinds[step], member[step], current, bias, readout
        )
        blocks = partial_value.reshape(GROUP_LOCAL, n_atm, width).transpose(1, 0, 2)
        tail = jnp.broadcast_to(energies[None, :, None], (n_atm, GROUP_LOCAL, LANES))
        shared = share_grads(jnp.concatenate([blocks, tail], axis=2), n_grp, n_atm)
        shared = shared.reshape(groups, width + LANES)
        jac = shared[:, :width]
        mismatch = targets[step] - shared[:, width]
        terms = row_terms(covariance, jac, n_atm) * (1.0 / forget_rate ** step)
        for age, (rows_old, cols_old, inverse_old) in enumerate(past):
            small = lax.dot_general(jac, cols_old, (((1,), (1,)), ((), ())), precision=precise)
            small = dot(small, inverse_old) * (1.0 / forget_rate ** (step - age))
            terms = terms - jnp.einsum("xy,nyp->nxp", small, rows_old, precision=precise)
        rows, cols = share_gains(terms, n_grp, n_atm)
        part = lax.dot_general(jac, cols, (((1,), (1,)), ((), ())), precision=precise)
        inverse = innovation_inverse(gather_atm(part, n_atm, 2))
        coefficient = dot(inverse, mismatch)
        change = dot(coefficient, cols).reshape(-1, current.shape[1])
        current = current + gather_atm(change, n_atm, 3).reshape(current.shape)
        past.append((rows, cols, inverse))
    left, right = [], []
    for age, (rows, cols, inverse) in enumerate(past):
        scaled = jnp.einsum("nxp,xy->npy", rows, inverse, precision=precise)
        left.append(scaled.reshape(-1, groups) * (1.0 / forget_rate ** (STEPS - age)))
        right.append(cols)
    covar = final_update(covariance, jnp.concatenate(left, axis=1), jnp.concatenate(right, axis=0))
    return (covar, current)


def solution(mesh):
    return jax.shard_map(
        body,
        mesh=mesh,
        in_specs=(
            P(None, ("grp", "atm"), None),
            P(None, ("grp", "atm")),
            P(None, ("grp", "atm")),
            P(),
            P(),
            P(),
            P(),
            P("grp", "atm"),
        ),
        out_specs=(P("grp", "atm"), P()),
        check_vma=False,
    )
```

```python
import functools
import jax
import jax.numpy as jnp
from jax import lax
from jax.experimental import pallas as pl
from jax.experimental.pallas import tpu as pltpu
from jax.sharding import PartitionSpec as P

GROUP_LOCAL = 8
STEPS = 2
CORES = 2
LANES = 128
CHUNKS = 2
PARTS = 1
HALVES = 2
RING = 4

forget_rate = 0.98
precise = lax.Precision.HIGHEST
MESH = pl.DeviceIdType.MESH
VM = pl.BlockSpec(memory_space=pltpu.VMEM)


def local_terms(atoms, kinds, member, weights, bias, readout):
    preact = jnp.dot(atoms, weights, precision=precise, preferred_element_type=jnp.float32) + bias
    hidden = jnp.tanh(preact)
    type_hot = (kinds[:, None] == jnp.arange(readout.shape[0])[None, :]).astype(jnp.float32)
    vectors = jnp.dot(type_hot, readout, precision=precise)
    atom_energy = jnp.sum(hidden * vectors, axis=1)
    slope = (1.0 - hidden * hidden) * vectors
    group_hot = (member[:, None] == jnp.arange(GROUP_LOCAL)[None, :]).astype(jnp.float32)
    energies = jnp.dot(atom_energy, group_hot, precision=precise)
    masked = atoms[:, None, :] * group_hot[:, :, None]
    grads = jnp.einsum("agi,ac->gic", masked, slope, precision=precise)
    return energies, grads.reshape(GROUP_LOCAL, -1)


def push(src, dst, sems, recvs, slot, target):
    copy = pltpu.make_async_remote_copy(
        src_ref=src, dst_ref=dst, send_sem=sems.at[slot], recv_sem=recvs.at[slot],
        device_id=target, device_id_type=MESH,
    )
    copy.start()
    return copy


def greet(targets):
    barrier = pltpu.get_barrier_semaphore()
    for target in targets:
        pl.semaphore_signal(barrier, inc=1, device_id=target, device_id_type=MESH)
    pl.semaphore_wait(barrier, len(targets))


def places(n_grp, n_atm):
    row, col = lax.axis_index("grp"), lax.axis_index("atm")
    n_z = n_grp // CORES
    z, core = row // CORES, lax.rem(row, CORES)
    plane = [lax.rem(col + d, n_atm) for d in range(1, n_atm)]
    column = [lax.rem(z + d, n_z) * CORES + core for d in range(1, n_z)]
    partner = z * CORES + (CORES - 1 - core)
    return row, col, z, core, plane, column, partner


def grads_kernel(n_grp, n_atm, x_ref, out_ref, got, a_s, a_r, b_s, b_r, f_s, f_r):
    row, col, z, core, plane, column, partner = places(n_grp, n_atm)
    greet([{"atm": p} for p in plane] + [{"grp": p} for p in column] + [{"grp": partner}])
    n_z = n_grp // CORES
    wide = x_ref.shape[2]
    middle = wide // 2 // LANES * LANES
    cuts = [pl.ds(0, middle), pl.ds(middle, wide - middle)]
    first, second, last = [], [], []
    for k, cut in enumerate(cuts):
        first.append([push(x_ref.at[p, :, cut], got.at[i, :, cut], a_s.at[k], a_r.at[k], i, {"atm": p}) for i, p in enumerate(plane)])
    for k, cut in enumerate(cuts):
        total = x_ref[col, :, cut]
        for i, copy in enumerate(first[k]):
            copy.wait_recv()
            total = total + got[i, :, cut]
        out_ref[row, :, cut] = total
        place = out_ref.at[row, :, cut]
        second.append([push(place, place, b_s.at[k], b_r.at[k], i, {"grp": p}) for i, p in enumerate(column)])
        last.append(push(place, place, f_s.at[k], f_r.at[k], len(column), {"grp": partner}))
    for k, cut in enumerate(cuts):
        for i, copy in enumerate(second[k]):
            copy.wait_recv()
            origin = lax.rem(z + n_z - (i + 1), n_z) * CORES + core
            place = out_ref.at[origin, :, cut]
            last.append(push(place, place, f_s.at[k], f_r.at[k], i, {"grp": partner}))
    for copy in last:
        copy.wait_recv()
    for copy in sum(first + second, last):
        copy.wait_send()


def share_grads(x, n_grp, n_atm):
    block = x.shape[1:]
    n_z = n_grp // CORES
    dma = pltpu.SemaphoreType.DMA
    return pl.pallas_call(
        functools.partial(grads_kernel, n_grp, n_atm),
        out_shape=jax.ShapeDtypeStruct((n_grp,) + block, jnp.float32),
        in_specs=[VM], out_specs=VM,
        scratch_shapes=[pltpu.VMEM((n_atm - 1,) + block, jnp.float32)]
        + [dma((2, n_atm - 1))] * 2 + [dma((2, n_z - 1))] * 2 + [dma((2, n_z))] * 2,
        compiler_params=pltpu.CompilerParams(collective_id=0, has_side_effects=True),
        name="share_grads",
    )(x)


def gains_kernel(n_grp, n_atm, half, t_ref, row_ref, col_ref, got, quarter,
                 a_s, a_r, r_s, r_r, b_s, b_r, c_s, c_r, f_s, f_r):
    row, col, z, core, plane, column, partner = places(n_grp, n_atm)
    greet([{"atm": p} for p in plane] + [{"grp": p} for p in column] + [{"grp": partner}])
    groups = t_ref.shape[1]
    chunk = groups // CHUNKS
    cuts = [pl.ds(k * chunk, chunk) for k in range(CHUNKS)]
    first, along, rows, across, last = [], [], [], [], []
    for k, cut in enumerate(cuts):
        first.append([push(t_ref.at[p, cut], got.at[i, cut], a_s.at[k], a_r.at[k], i, {"atm": p}) for i, p in enumerate(plane)])
    for k, cut in enumerate(cuts):
        total = t_ref[col, cut]
        for i, copy in enumerate(first[k]):
            copy.wait_recv()
            total = total + got[i, cut]
        quarter[z, cut] = total
        row_ref[col, cut] = total
        along.append([push(quarter.at[z, cut], quarter.at[z, cut], b_s.at[k], b_r.at[k], i, {"grp": p}) for i, p in enumerate(column)])
        rows.append([push(row_ref.at[col, cut], row_ref.at[col, cut], r_s.at[k], r_r.at[k], i, {"atm": p}) for i, p in enumerate(plane)])
    for k, cut in enumerate(cuts):
        for copy in along[k]:
            copy.wait_recv()
        across.append([
            push(quarter.at[pl.ds(p * half, half), cut], col_ref.at[core, col, :, cut], c_s.at[k], c_r.at[k], i, {"atm": p})
            for i, p in enumerate(plane)
        ])
        col_ref[core, col, :, cut] = quarter[pl.ds(col * half, half), cut]
        place = col_ref.at[core, col, :, cut]
        last.append([push(place, place, f_s.at[k], f_r.at[k], len(plane), {"grp": partner})])
    for k, cut in enumerate(cuts):
        for i, copy in enumerate(across[k]):
            copy.wait_recv()
            origin = lax.rem(col + n_atm - (i + 1), n_atm)
            place = col_ref.at[core, origin, :, cut]
            last[k].append(push(place, place, f_s.at[k], f_r.at[k], i, {"grp": partner}))
    for group in rows + last:
        for copy in group:
            copy.wait_recv()
    for group in first + along + rows + across + last:
        for copy in group:
            copy.wait_send()


def share_gains(t, n_grp, n_atm):
    _, groups, piece = t.shape
    per_col = n_grp // n_atm
    if n_grp % n_atm or per_col % CORES:
        mine = lax.psum(t, "atm")
        full = lax.all_gather(mine, "grp", axis=0).transpose(2, 0, 1, 3).reshape(groups, -1)
        width = full.shape[1] // n_atm
        return mine, lax.dynamic_slice_in_dim(full, lax.axis_index("atm") * width, width, 1)
    half = per_col // CORES
    n_z = n_grp // CORES
    dma = pltpu.SemaphoreType.DMA
    vm = lambda *lead: pltpu.VMEM(lead + (groups, piece), jnp.float32)
    rows, cols = pl.pallas_call(
        functools.partial(gains_kernel, n_grp, n_atm, half),
        out_shape=(
            jax.ShapeDtypeStruct((n_atm, groups, piece), jnp.float32),
            jax.ShapeDtypeStruct((CORES, n_atm, half, groups, piece), jnp.float32),
        ),
        in_specs=[VM], out_specs=(VM, VM),
        scratch_shapes=[vm(n_atm - 1), vm(n_z)]
        + [dma((CHUNKS, n_atm - 1))] * 4 + [dma((CHUNKS, n_z - 1))] * 2 + [dma((CHUNKS, n_atm - 1))] * 2 + [dma((CHUNKS, n_atm))] * 2,
        compiler_params=pltpu.CompilerParams(collective_id=1, has_side_effects=True),
        name="share_gains",
    )(t)
    return rows, cols.transpose(3, 2, 0, 1, 4).reshape(groups, -1)


def gather_kernel(n_atm, v_ref, out_ref, s, r):
    col = lax.axis_index("atm")
    plane = [lax.rem(col + d, n_atm) for d in range(1, n_atm)]
    greet([{"atm": p} for p in plane])
    copies = [push(v_ref, out_ref.at[col], s, r, i, {"atm": p}) for i, p in enumerate(plane)]
    out_ref[col] = v_ref[...]
    for copy in copies:
        copy.wait()


def gather_atm(v, n_atm, ident):
    return pl.pallas_call(
        functools.partial(gather_kernel, n_atm),
        out_shape=jax.ShapeDtypeStruct((n_atm,) + v.shape, jnp.float32),
        in_specs=[VM], out_specs=VM,
        scratch_shapes=[pltpu.SemaphoreType.DMA((n_atm - 1,))] * 2,
        compiler_params=pltpu.CompilerParams(collective_id=ident, has_side_effects=True),
        name="gather_atm%d" % ident,
    )(v)


def inverse_kernel(parts_ref, out_ref, work):
    size = out_ref.shape[0]
    total = parts_ref[0]
    for k in range(1, parts_ref.shape[0]):
        total = total + parts_ref[k]
    down = lax.broadcasted_iota(jnp.int32, (size, size), 0)
    over = lax.broadcasted_iota(jnp.int32, (size, size), 1)
    work[...] = 0.5 * (total + total.T) + jnp.where(down == over, forget_rate, 0.0)

    def sweep(k, carry):
        full = work[...]
        row = work[pl.ds(k, 1), :]
        column = jnp.sum(jnp.where(over == k, full, 0.0), axis=1, keepdims=True)
        pivot = 1.0 / jnp.sum(jnp.where(over[:1] == k, row, 0.0), axis=1, keepdims=True)
        row_part, col_part = row * pivot, column * pivot
        swept = full - column * row_part
        swept = jnp.where(down == k, row_part, swept)
        swept = jnp.where(over == k, col_part, swept)
        work[...] = jnp.where((down == k) & (over == k), -pivot, swept)
        return carry

    lax.fori_loop(0, size, sweep, 0)
    out_ref[...] = -work[...]


def innovation_inverse(parts):
    size = parts.shape[-1]
    return pl.pallas_call(
        inverse_kernel,
        out_shape=jax.ShapeDtypeStruct((size, size), jnp.float32),
        in_specs=[VM], out_specs=VM,
        scratch_shapes=[pltpu.VMEM((size, size), jnp.float32)],
        name="innovation_inverse",
    )(parts)


def split(value):
    high = value.astype(jnp.bfloat16)
    return high, (value - high.astype(jnp.float32)).astype(jnp.bfloat16)


def across(a, b, **options):
    return lax.dot_general(a, b, (((1,), (1,)), ((), ())), preferred_element_type=jnp.float32, **options)


def exact(a, b):
    return jnp.dot(a, b, precision=precise, preferred_element_type=jnp.float32)


def triple(a, b):
    high, low = split(a)
    high_b, low_b = split(b)
    left = jnp.concatenate([high, low, high], axis=1)
    right = jnp.concatenate([high_b, high_b, low_b], axis=0)
    return jnp.dot(left, right, preferred_element_type=jnp.float32)


def spd_sweep(value, start, stop, block=4):
    size = value.shape[0]
    down = lax.broadcasted_iota(jnp.int32, (size, size), 0)
    over = lax.broadcasted_iota(jnp.int32, (size, size), 1)
    for k in range(start, stop, block):
        own = range(block)
        columns = [jnp.broadcast_to(value[:, k + j:k + j + 1], (size, size)) for j in own]
        pivots = [[columns[j][k + i:k + i + 1, :] for j in own] for i in own]
        for q in own:
            turned = 1.0 / pivots[q][q]
            line = [turned if j == q else pivots[q][j] * turned for j in own]
            pivots = [
                line if i == q else [
                    -pivots[i][q] * turned if j == q else pivots[i][j] - pivots[i][q] * line[j] for j in own
                ] for i in own
            ]
        lines = []
        for i in own:
            line = value[k + i:k + i + 1, :]
            for j in own:
                line = jnp.where(over[:1] == k + j, 1.0 if i == j else 0.0, line)
            lines.append(line)
        lines = [sum(pivots[i][j] * lines[j] for j in own) for i in own]
        value = jnp.where((over >= k) & (over < k + block), 0.0, value)
        for j in own:
            value = value - columns[j] * lines[j]
        for j in own:
            value = jnp.where(down == k + j, lines[j], value)
    return value


def fused_kernel(n_grp, n_atm, *refs):
    small, refs = refs[:7], refs[7:]
    (p_hbm, p_ref, left_ref, right_ref, w_ref, *refs) = refs
    held, refs = refs[:7], refs[7:]
    (atoms_ref, kinds_ref, member_ref, targets_ref, weights_ref, bias_ref, readout_ref) = held
    (rows0, cols0, rows1, cols1, past_c, past_r,
     xt_ref, jpart, jgot, jall, both, tacc, tpart, tgot, jpiece, gpiece, quarter, cplane, cz, wplane, wz,
     p_sem, x_sem, j_s, j_r, z_s, z_r, f_s, f_r, i_s, i_r, t_s, t_r, c_s, c_r, d_s, d_r, w_s, w_r, v_s, v_r,
     gr_s, gr_r, gz_s, gz_r, ga_s, ga_r, gf_s, gf_r) = refs
    rows_all, cols_all = (rows0, rows1), (cols0, cols1)
    row, col, z, core, plane, column, partner = places(n_grp, n_atm)
    n_z = n_grp // CORES
    seat = core * n_atm + col
    seats = CORES * n_atm
    others = [lax.rem(seat + d, seats) for d in range(1, seats)]
    floor = [{"grp": z * CORES + o // n_atm, "atm": lax.rem(o, n_atm)} for o in others]
    groups = GROUP_LOCAL * n_grp
    rows, width = p_ref.shape
    features, units = weights_ref.shape
    local = jpart.shape[2] - 1
    chunk = local // PARTS
    span = chunk * units
    piece = rows // n_atm
    per = piece // units
    deep = min(span, 512)
    tall = min(piece, 512)
    steps = span // deep
    halves = [pl.ds(h * (groups // HALVES), groups // HALVES) for h in range(HALVES)]

    fetches = []
    for i, (source, target) in enumerate(zip(small, held)):
        fetch = pltpu.make_async_copy(source, target, x_sem.at[i])
        fetch.start()
        fetches.append(fetch)
    loads = []
    for k in range(PARTS):
        cut = pl.ds(k * span, span)
        load = pltpu.make_async_copy(p_hbm.at[:, cut], p_ref.at[:, cut], p_sem.at[k])
        load.start()
        loads.append(load)
    for fetch in fetches:
        fetch.wait()
    for step in range(STEPS):
        xt_ref[step] = atoms_ref[step].T

    current = weights_ref[...]
    inverses, sends, bulk = [], [], {}
    iota8 = lax.broadcasted_iota(jnp.int32, (GROUP_LOCAL, units), 0)

    def gains_first(step, h, here):
        mine = quarter.at[step, z, halves[h]]
        quarter[step, z, halves[h]] = here
        far = [push(mine, mine, gz_s.at[step, h], gz_r.at[step, h], i, {"grp": p}) for i, p in enumerate(column)]
        bulk[step, h] = [far, []]

    def gains_rows(step, h, here):
        place = rows_all[step].at[col, halves[h]]
        rows_all[step][col, halves[h]] = here
        bulk[step, h][1] += [push(place, place, gr_s.at[step, h], gr_r.at[step, h], i, {"atm": p}) for i, p in enumerate(plane)]

    def gains_second(step, h):
        half = halves[h]
        for copy in bulk[step, h][0]:
            copy.wait_recv()
        out = cols_all[step]
        place = out.at[core, col, half]
        swap = [push(quarter.at[step, p, half], place, ga_s.at[step, h], ga_r.at[step, h], i, {"atm": p}) for i, p in enumerate(plane)]
        out[core, col, half] = quarter[step, col, half]
        last = [push(place, place, gf_s.at[step, h], gf_r.at[step, h], len(plane), {"grp": partner})]
        bulk[step, h] += [swap, last]

    def gains_third(step, h):
        out = cols_all[step]
        for i, copy in enumerate(bulk[step, h][2]):
            copy.wait_recv()
            origin = lax.rem(col + n_atm - (i + 1), n_atm)
            place = out.at[core, origin, halves[h]]
            bulk[step, h][3].append(push(place, place, gf_s.at[step, h], gf_r.at[step, h], i, {"grp": partner}))

    def gains_near(step):
        for h in range(HALVES):
            for copy in bulk[step, h][1]:
                copy.wait_recv()

    def gains_last(step):
        for h in range(HALVES):
            for copy in bulk[step, h][3]:
                copy.wait_recv()

    for step in range(STEPS):
        if step == 1:
            for h in range(HALVES):
                gains_first(0, h, gpiece[0, halves[h]])

        x = atoms_ref[step]
        preact = exact(x, current) + bias_ref[...]
        hidden = jnp.tanh(preact)
        kinds_row = kinds_ref[step:step + 1, :].astype(jnp.float32)
        kinds_col = jnp.broadcast_to(kinds_row, (GROUP_LOCAL, kinds_row.shape[1])).T[:, :1]
        vectors = jnp.zeros_like(hidden)
        for kind in range(readout_ref.shape[0]):
            vectors = jnp.where(kinds_col == kind, readout_ref[kind:kind + 1, :], vectors)
        slope = (1.0 - hidden * hidden) * vectors
        slope_high, slope_low = split(slope)
        slope_both = jnp.concatenate([slope_high, slope_low], axis=1)
        n_own = x.shape[0]
        member_row = member_ref[step:step + 1, :]
        hot = (lax.broadcasted_iota(jnp.int32, (GROUP_LOCAL, n_own), 0) == member_row).astype(jnp.float32)
        energy = exact(hot, hidden * vectors)
        energy = jnp.broadcast_to(jnp.sum(energy, axis=1, keepdims=True), (GROUP_LOCAL, units))

        def grads(p):
            xs = xt_ref[step, pl.ds(p * local, local), :]
            high = xs.astype(jnp.bfloat16).astype(jnp.float32)
            pick = lambda v: (v[:, None, :] * hot[None]).reshape(local * GROUP_LOCAL, n_own).astype(jnp.bfloat16)
            one = jnp.dot(pick(high), slope_both, preferred_element_type=jnp.float32)
            two = jnp.dot(pick(xs - high), slope_high, preferred_element_type=jnp.float32)
            total = one[:, :units] + one[:, units:] + two
            jpart[step, p, :local] = total.reshape(local, GROUP_LOCAL, units)
            jpart[step, p, local] = energy

        if step == 0:
            greet(floor + [{"grp": p} for p in column])
        cuts = [pl.ds(k * chunk, chunk + (1 if k == PARTS - 1 else 0)) for k in range(PARTS)]
        first = [[] for _ in cuts]
        for i, p in enumerate(plane):
            grads(p)
            for k, cut in enumerate(cuts):
                first[k].append(push(jpart.at[step, p, cut], jgot.at[step, i, cut], j_s.at[step, k], j_r.at[step, k], i, {"atm": p}))
        grads(col)
        if step == 1:
            for copy in early_sends:
                copy.wait_send()
        second, third = [], []
        for k, cut in enumerate(cuts):
            total = jpart[step, col, cut]
            for i, copy in enumerate(first[k]):
                copy.wait_recv()
                total = total + jgot[step, i, cut]
            jall[step, row, cut] = total
            place = jall.at[step, row, cut]
            second.append([push(place, place, z_s.at[step, k], z_r.at[step, k], i, {"grp": p}) for i, p in enumerate(column)])
            third.append([push(place, place, f_s.at[step, k], f_r.at[step, k], len(column), {"grp": partner})])
        sends += sum(first + second, [])

        if step == 1:
            for h in range(HALVES):
                gains_second(0, h)
                gains_rows(0, h, gpiece[0, halves[h]])

        def forward(k):
            for i, copy in enumerate(second[k]):
                copy.wait_recv()
                origin = lax.rem(z + n_z - (i + 1), n_z) * CORES + core
                place = jall.at[step, origin, cuts[k]]
                third[k].append(push(place, place, f_s.at[step, k], f_r.at[step, k], i, {"grp": partner}))

        def product(at, over):
            high, low = split(p_ref[pl.ds(at, tall), pl.ds(over, deep)])
            right = both[step, :, pl.ds(over, deep)]
            return across(high, right) + across(low, right)

        def some_rows(k, start, stop):
            def add(t, carry):
                at = pl.multiple_of(t // steps * tall, tall)
                over = pl.multiple_of(k * span + lax.rem(t, steps) * deep, deep)
                tacc[pl.ds(at, tall), :] += product(at, over)
                return carry
            lax.fori_loop(start * steps, stop * steps, add, 0)

        def last_rows(i, carry):
            p = lax.rem(col + 1 + i, n_atm)

            def add(t, carry):
                at = pl.multiple_of(p * piece + t // steps * tall, tall)
                over = pl.multiple_of((PARTS - 1) * span + lax.rem(t, steps) * deep, deep)
                tacc[pl.ds(at, tall), :] += product(at, over)
                return carry
            lax.fori_loop(0, piece // tall * steps, add, 0)
            value = tacc[pl.ds(pl.multiple_of(p * piece, piece), piece), :].T
            tpart[step, p] = value[:groups] + value[groups:]

            @pl.when(i < n_atm - 1)
            def _():
                for h in range(HALVES):
                    spread(h, i).start()
            return carry

        def spread(h, i):
            p = lax.rem(col + 1 + i, n_atm)
            return pltpu.make_async_remote_copy(
                src_ref=tpart.at[step, p, halves[h]], dst_ref=tgot.at[step, i, halves[h]],
                send_sem=t_s.at[step, h, i], recv_sem=t_r.at[step, h, i], device_id={"atm": p}, device_id_type=MESH)

        tacc[...] = jnp.zeros_like(tacc)
        scatter = [[spread(h, i) for i in range(n_atm - 1)] for h in range(HALVES)]
        forward(0)
        for k in range(PARTS):
            for copy in third[k]:
                copy.wait_recv()
            sends += third[k]
            for i in range(k * chunk, (k + 1) * chunk):
                high, low = split(jall[step, :, i].reshape(groups, units))
                both[step, :groups, i * units:(i + 1) * units] = high
                both[step, groups:, i * units:(i + 1) * units] = low
            if step == 0:
                loads[k].wait()
            if k < PARTS - 1:
                some_rows(k, 0, rows // tall // 2)
                forward(k + 1)
                some_rows(k, rows // tall // 2, rows // tall)
            else:
                inner = local // CORES
                window = lambda p: pl.ds(core * inner + p * per, per)
                jp_copies = [pltpu.make_async_remote_copy(
                    src_ref=jall.at[step, :, window(p)], dst_ref=jpiece.at[step], send_sem=i_s.at[step, i], recv_sem=i_r.at[step],
                    device_id={"atm": p}, device_id_type=MESH) for i, p in enumerate(plane)]

                @pl.when(col == z)
                def _():
                    for copy in jp_copies:
                        copy.start()
                    jpiece[step] = jall[step, :, window(col)]

                lax.fori_loop(0, n_atm, last_rows, 0)
        for h, half in enumerate(halves):
            sends += scatter[h]
            gain = tpart[step, col, half]
            for i, copy in enumerate(scatter[h]):
                copy.wait_recv()
                gain = gain + tgot[step, i, half]
            gpiece[step, half] = gain
            if step == STEPS - 1:
                gains_first(step, h, gain)
                gains_rows(step, h, gain)
        gain = gpiece[step]

        @pl.when(col != z)
        def _():
            jp_copies[0].wait_recv()

        @pl.when(col == z)
        def _():
            for copy in jp_copies:
                copy.wait_send()

        jp = jnp.concatenate([jpiece[step, :, j].reshape(groups, units) for j in range(per)], axis=1)
        stack = gain if step == 0 else jnp.concatenate([gain] + [gpiece[s] for s in range(step)], axis=0)
        terms = across(jp, stack, precision=precise)
        if step == 0:
            terms = jnp.concatenate([terms[:groups // 2], terms[groups // 2:]], axis=1)
        size = pl.ds(0, terms.shape[0])
        cplane[step, seat, size] = terms
        place = cplane.at[step, seat, size]
        hop = [push(place, place, c_s.at[step], c_r.at[step], i, d) for i, d in enumerate(floor)]
        if step == 1:
            for h in range(HALVES):
                gains_third(0, h)
        for copy in hop:
            copy.wait_recv()
        terms = cplane[step, 0, size]
        for i in range(1, seats):
            terms = terms + cplane[step, i, size]
        cz[step, z, size] = terms
        place = cz.at[step, z, size]
        skip = [push(place, place, d_s.at[step], d_r.at[step], i, {"grp": p}) for i, p in enumerate(column)]
        for copy in skip:
            copy.wait_recv()
        sends += hop + skip
        terms = cz[step, 0, size]
        for i in range(1, n_z):
            terms = terms + cz[step, i, size]
        if step == 0:
            curve = jnp.concatenate([terms[:, :groups], terms[:, groups:]], axis=0)
        else:
            cross = terms[:, groups:]
            early = exact(cross, inverses[0])
            curve = (terms[:, :groups] - across(early, cross, precision=precise)) * (1.0 / forget_rate)
        down = lax.broadcasted_iota(jnp.int32, (groups, groups), 0)
        over = lax.broadcasted_iota(jnp.int32, (groups, groups), 1)
        inverse = 0.5 * (curve + curve.T) + jnp.where(down == over, forget_rate, 0.0)
        inverse = spd_sweep(inverse, 0, groups // 2)
        if step == 1:
            gains_second(step, 0)
        inverse = spd_sweep(inverse, groups // 2, groups)
        if step == 1:
            for h in range(1, HALVES):
                gains_second(step, h)
        inverses.append(inverse)
        if step == 1:
            gain = (gain - exact(early, gpiece[0])) * (1.0 / forget_rate)

        predicted = jall[step, :, local].reshape(groups, units).T
        mismatch = jnp.broadcast_to(targets_ref[step:step + 1, :], (GROUP_LOCAL, groups)) - predicted[:GROUP_LOCAL]
        change = exact(exact(mismatch, inverse), gain)
        turn = lax.rem(iota8, per)
        mine = change[:, :units]
        for j in range(1, per):
            mine = jnp.where(turn == j, change[:, j * units:(j + 1) * units], mine)
        wplane[step, seat] = mine
        place = wplane.at[step, seat]
        hop = [push(place, place, w_s.at[step], w_r.at[step], i, d) for i, d in enumerate(floor)]
        if step == 1:
            gains_third(step, 0)
        for copy in hop:
            copy.wait_recv()
        fold = GROUP_LOCAL // per
        for m in range(seats // fold):
            dense = wplane[step, m * fold]
            for j in range(1, fold):
                dense = jnp.where(iota8 >= j * per, wplane[step, m * fold + j], dense)
            wz[step, z, m * GROUP_LOCAL:(m + 1) * GROUP_LOCAL] = dense
        place = wz.at[step, z]
        skip = [push(place, place, v_s.at[step], v_r.at[step], i, {"grp": p}) for i, p in enumerate(column)]
        sends += hop + skip
        if step == 1:
            for h in range(1, HALVES):
                gains_third(step, h)
            gains_near(0)
            gains_last(0)
            scaled = inverses[0] * (1.0 / forget_rate ** STEPS)
            for b in range(seats):
                high, low = split(triple(scaled, cols0[b // n_atm, b % n_atm]))
                right_ref[:groups, b * piece:(b + 1) * piece] = high
                right_ref[STEPS * groups:(STEPS + 1) * groups, b * piece:(b + 1) * piece] = low
            past = early * (1.0 / forget_rate)
            for b in range(seats):
                past_c[b] = triple(past, cols0[b // n_atm, b % n_atm])
            gains_near(1)
            for p in range(n_atm):
                later = rows1[p] * (1.0 / forget_rate) - triple(past, rows0[p])
                high, low = split(jnp.concatenate([rows0[p], later], axis=0).T)
                left_ref[p * piece:(p + 1) * piece, :] = jnp.concatenate([high, low], axis=1)
        for copy in skip:
            copy.wait_recv()
        current = current + wz[step].reshape(features, units)
        if step == 0:
            early_sends, sends = sends, []

    w_ref[...] = current
    for part in bulk.values():
        sends += sum(part[:3], [])
    for copy in sends:
        copy.wait_send()
    gains_last(1)
    scaled = inverses[1] * (1.0 / forget_rate)
    for b in range(seats):
        later = cols1[b // n_atm, b % n_atm] * (1.0 / forget_rate) - past_c[b]
        high, low = split(triple(scaled, later))
        right_ref[groups:STEPS * groups, b * piece:(b + 1) * piece] = high
        right_ref[(STEPS + 1) * groups:, b * piece:(b + 1) * piece] = low
    for part in bulk.values():
        for copy in part[3]:
            copy.wait_send()


def fused(*args, n_grp, n_atm):
    atoms, kinds, member, targets, weights, bias, readout, covariance = args
    small = [atoms, kinds, member, targets, weights, bias.reshape(1, -1), readout]
    rows, width = covariance.shape
    units = weights.shape[1]
    groups = GROUP_LOCAL * n_grp
    n_z = n_grp // CORES
    seats = CORES * n_atm
    local = width // units
    piece = rows // n_atm
    per = piece // units
    block = (local + 1, GROUP_LOCAL, units)
    f32 = jnp.float32
    dma = pltpu.SemaphoreType.DMA
    vm = lambda *shape: pltpu.VMEM(shape, f32)
    pair = lambda *shape: [dma((STEPS,) + shape)] * 2
    out_shape = (
        vm(rows, width),
        jax.ShapeDtypeStruct((rows, 2 * STEPS * groups), jnp.bfloat16),
        jax.ShapeDtypeStruct((2 * STEPS * groups, width), jnp.bfloat16),
        jax.ShapeDtypeStruct(weights.shape, f32),
    )
    HBM = pl.BlockSpec(memory_space=pltpu.HBM)
    covar, *outs = pl.pallas_call(
        functools.partial(fused_kernel, n_grp, n_atm),
        out_shape=out_shape,
        in_specs=[HBM] * 8,
        out_specs=(VM,) * len(out_shape),
        scratch_shapes=[pltpu.VMEM(v.shape, v.dtype) for v in small]
        + [vm(n_atm, groups, piece), vm(CORES, n_atm, groups, piece)] * 2
        + [
            vm(seats, groups, piece), vm(n_atm, groups, piece),
            vm(STEPS, atoms.shape[2], atoms.shape[1]),
            vm(STEPS, n_atm, *block), vm(STEPS, n_atm - 1, *block), vm(STEPS, n_grp, *block),
            pltpu.VMEM((STEPS, 2 * groups, width), jnp.bfloat16),
            vm(rows, 2 * groups),
            vm(STEPS, n_atm, groups, piece), vm(STEPS, n_atm - 1, groups, piece),
            vm(STEPS, n_grp, per, GROUP_LOCAL, units), vm(STEPS, groups, piece), vm(STEPS, n_z, groups, piece),
            vm(STEPS, seats, groups, STEPS * groups), vm(STEPS, n_z, groups, STEPS * groups),
            vm(STEPS, seats, GROUP_LOCAL, units), vm(STEPS, n_z, seats * per, units),
            dma((PARTS,)), dma((len(small),)),
        ] + pair(PARTS, n_atm - 1) + pair(PARTS, n_z - 1) + pair(PARTS, n_z)
        + [dma((STEPS, n_atm - 1)), dma((STEPS,))] + pair(HALVES, n_atm - 1)
        + pair(seats - 1) + pair(n_z - 1) + pair(seats - 1) + pair(n_z - 1)
        + pair(HALVES, n_atm - 1) + pair(HALVES, n_z - 1) + pair(HALVES, n_atm - 1) + pair(HALVES, n_atm),
        compiler_params=pltpu.CompilerParams(collective_id=4, has_side_effects=True, vmem_limit_bytes=30 << 20),
        name="updates",
    )(*small, covariance)
    return [pltpu.with_memory_space_constraint(covar, pltpu.VMEM), *outs]


def finish_kernel(tile, p_ref, left_ref, right_ref, w_in, out_ref, w_out, ring, sem):
    w_out[...] = w_in[...]
    rows, width = p_ref.shape
    depth = left_ref.shape[1] // 2
    part = min(width, 512)

    def leave(t):
        slot = lax.rem(t, RING)
        return pltpu.make_async_copy(ring.at[slot], out_ref.at[pl.ds(pl.multiple_of(t * tile, tile), tile)], sem.at[slot])

    def one(t, carry):
        @pl.when(t >= RING)
        def _():
            leave(t - RING).wait()

        here = pl.ds(pl.multiple_of(t * tile, tile), tile)
        slot = lax.rem(t, RING)
        high, low = left_ref[here, :depth], left_ref[here, depth:]
        twice = jnp.concatenate([high, high], axis=1)
        for k in range(0, width, part):
            cut = slice(k, k + part)
            down = jnp.dot(twice, right_ref[:, cut], preferred_element_type=jnp.float32)
            down = down + jnp.dot(low, right_ref[:depth, cut], preferred_element_type=jnp.float32)
            ring[slot, :, cut] = p_ref[here, cut] * (1.0 / forget_rate ** STEPS) - down
        leave(t).start()
        return carry

    lax.fori_loop(0, rows // tile, one, 0)
    for t in range(rows // tile - RING, rows // tile):
        leave(t).wait()


def finish(covar, left, right, weights):
    rows, width = covar.shape
    tile = min(rows // RING, 128)
    return pl.pallas_call(
        functools.partial(finish_kernel, tile),
        out_shape=(jax.ShapeDtypeStruct((rows, width), jnp.float32), jax.ShapeDtypeStruct(weights.shape, jnp.float32)),
        in_specs=[VM] * 4,
        out_specs=(pl.BlockSpec(memory_space=pltpu.HBM), VM),
        scratch_shapes=[pltpu.VMEM((RING, tile, width), jnp.float32), pltpu.SemaphoreType.DMA((RING,))],
        compiler_params=pltpu.CompilerParams(vmem_limit_bytes=30 << 20),
        name="finish",
    )(covar, left, right, weights)


def terms_kernel(groups, jac_ref, p_ref, out_ref, both):
    @pl.when(pl.program_id(0) == 0)
    def _():
        jac = jac_ref[...]
        high = jac.astype(jnp.bfloat16).astype(jnp.float32)
        both[...] = jnp.concatenate([high, jac - high], axis=0).T.astype(jnp.bfloat16)

    high, low = split(p_ref[...])
    one = jnp.dot(high, both[...], preferred_element_type=jnp.float32)
    two = jnp.dot(low, both[...], preferred_element_type=jnp.float32)
    one = one.T
    out_ref[0] = one[:groups] + one[groups:] + two.T[:groups]


def row_terms(covar, jac, n_atm):
    rows, width = covar.shape
    groups = jac.shape[0]
    piece = rows // n_atm
    tile = min(piece, 256)
    per = piece // tile
    return pl.pallas_call(
        functools.partial(terms_kernel, groups),
        grid=(rows // tile,),
        out_shape=jax.ShapeDtypeStruct((n_atm, groups, piece), jnp.float32),
        in_specs=[
            pl.BlockSpec((groups, width), lambda i: (0, 0)),
            pl.BlockSpec((tile, width), lambda i: (i, 0)),
        ],
        out_specs=pl.BlockSpec((1, groups, tile), lambda i: (i // per, 0, lax.rem(i, per))),
        scratch_shapes=[pltpu.VMEM((width, 2 * groups), jnp.bfloat16)],
        compiler_params=pltpu.CompilerParams(vmem_limit_bytes=48 << 20),
        name="row_terms",
    )(jac, covar)


def update_kernel(scale, left_ref, right_ref, p_ref, out_ref, right):
    @pl.when(pl.program_id(0) == 0)
    def _():
        high, low = split(right_ref[...])
        right[...] = jnp.concatenate([high, high, low], axis=0)

    high, low = split(left_ref[...])
    left = jnp.concatenate([high, low, high], axis=1)
    width = p_ref.shape[1]
    part = min(width, 512)
    for k in range(0, width, part):
        down = jnp.dot(left, right[:, k:k + part], preferred_element_type=jnp.float32)
        out_ref[:, k:k + part] = p_ref[:, k:k + part] * scale - down


def final_update(covar, left, right):
    rows, width = covar.shape
    depth = left.shape[1]
    tile = min(rows, 256)
    return pl.pallas_call(
        functools.partial(update_kernel, 1.0 / forget_rate ** STEPS),
        grid=(rows // tile,),
        out_shape=jax.ShapeDtypeStruct((rows, width), jnp.float32),
        in_specs=[
            pl.BlockSpec((tile, depth), lambda i: (i, 0)),
            pl.BlockSpec((depth, width), lambda i: (0, 0)),
            pl.BlockSpec((tile, width), lambda i: (i, 0)),
        ],
        out_specs=pl.BlockSpec((tile, width), lambda i: (i, 0)),
        scratch_shapes=[pltpu.VMEM((3 * depth, width), jnp.bfloat16)],
        compiler_params=pltpu.CompilerParams(vmem_limit_bytes=48 << 20),
        name="final_update",
    )(left, right, covar)


def body(atoms, kinds, member, targets, weights, bias, readout, covariance):
    n_grp, n_atm = lax.axis_size("grp"), lax.axis_size("atm")
    rows, width = covariance.shape
    units = weights.shape[1]
    if n_grp == CORES * n_atm and rows % (n_atm * units) == 0 and GROUP_LOCAL % (rows // (n_atm * units)) == 0:
        return finish(*fused(
            atoms, kinds, member, targets, weights, bias, readout, covariance, n_grp=n_grp, n_atm=n_atm
        ))
    groups = GROUP_LOCAL * n_grp
    dot = functools.partial(jnp.dot, precision=precise)
    current = weights
    past = []
    for step in range(STEPS):
        energies, partial_value = local_terms(
            atoms[step], kinds[step], member[step], current, bias, readout
        )
        blocks = partial_value.reshape(GROUP_LOCAL, n_atm, width).transpose(1, 0, 2)
        tail = jnp.broadcast_to(energies[None, :, None], (n_atm, GROUP_LOCAL, LANES))
        shared = share_grads(jnp.concatenate([blocks, tail], axis=2), n_grp, n_atm)
        shared = shared.reshape(groups, width + LANES)
        jac = shared[:, :width]
        mismatch = targets[step] - shared[:, width]
        terms = row_terms(covariance, jac, n_atm) * (1.0 / forget_rate ** step)
        for age, (rows_old, cols_old, inverse_old) in enumerate(past):
            small = lax.dot_general(jac, cols_old, (((1,), (1,)), ((), ())), precision=precise)
            small = dot(small, inverse_old) * (1.0 / forget_rate ** (step - age))
            terms = terms - jnp.einsum("xy,nyp->nxp", small, rows_old, precision=precise)
        rows, cols = share_gains(terms, n_grp, n_atm)
        part = lax.dot_general(jac, cols, (((1,), (1,)), ((), ())), precision=precise)
        inverse = innovation_inverse(gather_atm(part, n_atm, 2))
        coefficient = dot(inverse, mismatch)
        change = dot(coefficient, cols).reshape(-1, current.shape[1])
        current = current + gather_atm(change, n_atm, 3).reshape(current.shape)
        past.append((rows, cols, inverse))
    left, right = [], []
    for age, (rows, cols, inverse) in enumerate(past):
        scaled = jnp.einsum("nxp,xy->npy", rows, inverse, precision=precise)
        left.append(scaled.reshape(-1, groups) * (1.0 / forget_rate ** (STEPS - age)))
        right.append(cols)
    covar = final_update(covariance, jnp.concatenate(left, axis=1), jnp.concatenate(right, axis=0))
    return (covar, current)


def solution(mesh):
    return jax.shard_map(
        body,
        mesh=mesh,
        in_specs=(
            P(None, ("grp", "atm"), None),
            P(None, ("grp", "atm")),
            P(None, ("grp", "atm")),
            P(),
            P(),
            P(),
            P(),
            P("grp", "atm"),
        ),
        out_specs=(P("grp", "atm"), P()),
        check_vma=False,
    )
```

```python
import functools
import jax
import jax.numpy as jnp
from jax import lax
from jax.experimental import pallas as pl
from jax.experimental.pallas import tpu as pltpu
from jax.sharding import PartitionSpec as P

GROUP_LOCAL = 8
STEPS = 2
CORES = 2
LANES = 128
CHUNKS = 2
PARTS = 1
HALVES = 1
RING = 4

forget_rate = 0.98
precise = lax.Precision.HIGHEST
MESH = pl.DeviceIdType.MESH
VM = pl.BlockSpec(memory_space=pltpu.VMEM)


def local_terms(atoms, kinds, member, weights, bias, readout):
    preact = jnp.dot(atoms, weights, precision=precise, preferred_element_type=jnp.float32) + bias
    hidden = jnp.tanh(preact)
    type_hot = (kinds[:, None] == jnp.arange(readout.shape[0])[None, :]).astype(jnp.float32)
    vectors = jnp.dot(type_hot, readout, precision=precise)
    atom_energy = jnp.sum(hidden * vectors, axis=1)
    slope = (1.0 - hidden * hidden) * vectors
    group_hot = (member[:, None] == jnp.arange(GROUP_LOCAL)[None, :]).astype(jnp.float32)
    energies = jnp.dot(atom_energy, group_hot, precision=precise)
    masked = atoms[:, None, :] * group_hot[:, :, None]
    grads = jnp.einsum("agi,ac->gic", masked, slope, precision=precise)
    return energies, grads.reshape(GROUP_LOCAL, -1)


def push(src, dst, sems, recvs, slot, target):
    copy = pltpu.make_async_remote_copy(
        src_ref=src, dst_ref=dst, send_sem=sems.at[slot], recv_sem=recvs.at[slot],
        device_id=target, device_id_type=MESH,
    )
    copy.start()
    return copy


def greet(targets):
    barrier = pltpu.get_barrier_semaphore()
    for target in targets:
        pl.semaphore_signal(barrier, inc=1, device_id=target, device_id_type=MESH)
    pl.semaphore_wait(barrier, len(targets))


def places(n_grp, n_atm):
    row, col = lax.axis_index("grp"), lax.axis_index("atm")
    n_z = n_grp // CORES
    z, core = row // CORES, lax.rem(row, CORES)
    plane = [lax.rem(col + d, n_atm) for d in range(1, n_atm)]
    column = [lax.rem(z + d, n_z) * CORES + core for d in range(1, n_z)]
    partner = z * CORES + (CORES - 1 - core)
    return row, col, z, core, plane, column, partner


def grads_kernel(n_grp, n_atm, x_ref, out_ref, got, a_s, a_r, b_s, b_r, f_s, f_r):
    row, col, z, core, plane, column, partner = places(n_grp, n_atm)
    greet([{"atm": p} for p in plane] + [{"grp": p} for p in column] + [{"grp": partner}])
    n_z = n_grp // CORES
    wide = x_ref.shape[2]
    middle = wide // 2 // LANES * LANES
    cuts = [pl.ds(0, middle), pl.ds(middle, wide - middle)]
    first, second, last = [], [], []
    for k, cut in enumerate(cuts):
        first.append([push(x_ref.at[p, :, cut], got.at[i, :, cut], a_s.at[k], a_r.at[k], i, {"atm": p}) for i, p in enumerate(plane)])
    for k, cut in enumerate(cuts):
        total = x_ref[col, :, cut]
        for i, copy in enumerate(first[k]):
            copy.wait_recv()
            total = total + got[i, :, cut]
        out_ref[row, :, cut] = total
        place = out_ref.at[row, :, cut]
        second.append([push(place, place, b_s.at[k], b_r.at[k], i, {"grp": p}) for i, p in enumerate(column)])
        last.append(push(place, place, f_s.at[k], f_r.at[k], len(column), {"grp": partner}))
    for k, cut in enumerate(cuts):
        for i, copy in enumerate(second[k]):
            copy.wait_recv()
            origin = lax.rem(z + n_z - (i + 1), n_z) * CORES + core
            place = out_ref.at[origin, :, cut]
            last.append(push(place, place, f_s.at[k], f_r.at[k], i, {"grp": partner}))
    for copy in last:
        copy.wait_recv()
    for copy in sum(first + second, last):
        copy.wait_send()


def share_grads(x, n_grp, n_atm):
    block = x.shape[1:]
    n_z = n_grp // CORES
    dma = pltpu.SemaphoreType.DMA
    return pl.pallas_call(
        functools.partial(grads_kernel, n_grp, n_atm),
        out_shape=jax.ShapeDtypeStruct((n_grp,) + block, jnp.float32),
        in_specs=[VM], out_specs=VM,
        scratch_shapes=[pltpu.VMEM((n_atm - 1,) + block, jnp.float32)]
        + [dma((2, n_atm - 1))] * 2 + [dma((2, n_z - 1))] * 2 + [dma((2, n_z))] * 2,
        compiler_params=pltpu.CompilerParams(collective_id=0, has_side_effects=True),
        name="share_grads",
    )(x)


def gains_kernel(n_grp, n_atm, half, t_ref, row_ref, col_ref, got, quarter,
                 a_s, a_r, r_s, r_r, b_s, b_r, c_s, c_r, f_s, f_r):
    row, col, z, core, plane, column, partner = places(n_grp, n_atm)
    greet([{"atm": p} for p in plane] + [{"grp": p} for p in column] + [{"grp": partner}])
    groups = t_ref.shape[1]
    chunk = groups // CHUNKS
    cuts = [pl.ds(k * chunk, chunk) for k in range(CHUNKS)]
    first, along, rows, across, last = [], [], [], [], []
    for k, cut in enumerate(cuts):
        first.append([push(t_ref.at[p, cut], got.at[i, cut], a_s.at[k], a_r.at[k], i, {"atm": p}) for i, p in enumerate(plane)])
    for k, cut in enumerate(cuts):
        total = t_ref[col, cut]
        for i, copy in enumerate(first[k]):
            copy.wait_recv()
            total = total + got[i, cut]
        quarter[z, cut] = total
        row_ref[col, cut] = total
        along.append([push(quarter.at[z, cut], quarter.at[z, cut], b_s.at[k], b_r.at[k], i, {"grp": p}) for i, p in enumerate(column)])
        rows.append([push(row_ref.at[col, cut], row_ref.at[col, cut], r_s.at[k], r_r.at[k], i, {"atm": p}) for i, p in enumerate(plane)])
    for k, cut in enumerate(cuts):
        for copy in along[k]:
            copy.wait_recv()
        across.append([
            push(quarter.at[pl.ds(p * half, half), cut], col_ref.at[core, col, :, cut], c_s.at[k], c_r.at[k], i, {"atm": p})
            for i, p in enumerate(plane)
        ])
        col_ref[core, col, :, cut] = quarter[pl.ds(col * half, half), cut]
        place = col_ref.at[core, col, :, cut]
        last.append([push(place, place, f_s.at[k], f_r.at[k], len(plane), {"grp": partner})])
    for k, cut in enumerate(cuts):
        for i, copy in enumerate(across[k]):
            copy.wait_recv()
            origin = lax.rem(col + n_atm - (i + 1), n_atm)
            place = col_ref.at[core, origin, :, cut]
            last[k].append(push(place, place, f_s.at[k], f_r.at[k], i, {"grp": partner}))
    for group in rows + last:
        for copy in group:
            copy.wait_recv()
    for group in first + along + rows + across + last:
        for copy in group:
            copy.wait_send()


def share_gains(t, n_grp, n_atm):
    _, groups, piece = t.shape
    per_col = n_grp // n_atm
    if n_grp % n_atm or per_col % CORES:
        mine = lax.psum(t, "atm")
        full = lax.all_gather(mine, "grp", axis=0).transpose(2, 0, 1, 3).reshape(groups, -1)
        width = full.shape[1] // n_atm
        return mine, lax.dynamic_slice_in_dim(full, lax.axis_index("atm") * width, width, 1)
    half = per_col // CORES
    n_z = n_grp // CORES
    dma = pltpu.SemaphoreType.DMA
    vm = lambda *lead: pltpu.VMEM(lead + (groups, piece), jnp.float32)
    rows, cols = pl.pallas_call(
        functools.partial(gains_kernel, n_grp, n_atm, half),
        out_shape=(
            jax.ShapeDtypeStruct((n_atm, groups, piece), jnp.float32),
            jax.ShapeDtypeStruct((CORES, n_atm, half, groups, piece), jnp.float32),
        ),
        in_specs=[VM], out_specs=(VM, VM),
        scratch_shapes=[vm(n_atm - 1), vm(n_z)]
        + [dma((CHUNKS, n_atm - 1))] * 4 + [dma((CHUNKS, n_z - 1))] * 2 + [dma((CHUNKS, n_atm - 1))] * 2 + [dma((CHUNKS, n_atm))] * 2,
        compiler_params=pltpu.CompilerParams(collective_id=1, has_side_effects=True),
        name="share_gains",
    )(t)
    return rows, cols.transpose(3, 2, 0, 1, 4).reshape(groups, -1)


def gather_kernel(n_atm, v_ref, out_ref, s, r):
    col = lax.axis_index("atm")
    plane = [lax.rem(col + d, n_atm) for d in range(1, n_atm)]
    greet([{"atm": p} for p in plane])
    copies = [push(v_ref, out_ref.at[col], s, r, i, {"atm": p}) for i, p in enumerate(plane)]
    out_ref[col] = v_ref[...]
    for copy in copies:
        copy.wait()


def gather_atm(v, n_atm, ident):
    return pl.pallas_call(
        functools.partial(gather_kernel, n_atm),
        out_shape=jax.ShapeDtypeStruct((n_atm,) + v.shape, jnp.float32),
        in_specs=[VM], out_specs=VM,
        scratch_shapes=[pltpu.SemaphoreType.DMA((n_atm - 1,))] * 2,
        compiler_params=pltpu.CompilerParams(collective_id=ident, has_side_effects=True),
        name="gather_atm%d" % ident,
    )(v)


def inverse_kernel(parts_ref, out_ref, work):
    size = out_ref.shape[0]
    total = parts_ref[0]
    for k in range(1, parts_ref.shape[0]):
        total = total + parts_ref[k]
    down = lax.broadcasted_iota(jnp.int32, (size, size), 0)
    over = lax.broadcasted_iota(jnp.int32, (size, size), 1)
    work[...] = 0.5 * (total + total.T) + jnp.where(down == over, forget_rate, 0.0)

    def sweep(k, carry):
        full = work[...]
        row = work[pl.ds(k, 1), :]
        column = jnp.sum(jnp.where(over == k, full, 0.0), axis=1, keepdims=True)
        pivot = 1.0 / jnp.sum(jnp.where(over[:1] == k, row, 0.0), axis=1, keepdims=True)
        row_part, col_part = row * pivot, column * pivot
        swept = full - column * row_part
        swept = jnp.where(down == k, row_part, swept)
        swept = jnp.where(over == k, col_part, swept)
        work[...] = jnp.where((down == k) & (over == k), -pivot, swept)
        return carry

    lax.fori_loop(0, size, sweep, 0)
    out_ref[...] = -work[...]


def innovation_inverse(parts):
    size = parts.shape[-1]
    return pl.pallas_call(
        inverse_kernel,
        out_shape=jax.ShapeDtypeStruct((size, size), jnp.float32),
        in_specs=[VM], out_specs=VM,
        scratch_shapes=[pltpu.VMEM((size, size), jnp.float32)],
        name="innovation_inverse",
    )(parts)


def split(value):
    high = value.astype(jnp.bfloat16)
    return high, (value - high.astype(jnp.float32)).astype(jnp.bfloat16)


def across(a, b, **options):
    return lax.dot_general(a, b, (((1,), (1,)), ((), ())), preferred_element_type=jnp.float32, **options)


def exact(a, b):
    return jnp.dot(a, b, precision=precise, preferred_element_type=jnp.float32)


def triple(a, b):
    high, low = split(a)
    high_b, low_b = split(b)
    left = jnp.concatenate([high, low, high], axis=1)
    right = jnp.concatenate([high_b, high_b, low_b], axis=0)
    return jnp.dot(left, right, preferred_element_type=jnp.float32)


def spd_sweep(value, start, stop, block=4):
    size = value.shape[0]
    down = lax.broadcasted_iota(jnp.int32, (size, size), 0)
    over = lax.broadcasted_iota(jnp.int32, (size, size), 1)
    for k in range(start, stop, block):
        own = range(block)
        columns = [jnp.broadcast_to(value[:, k + j:k + j + 1], (size, size)) for j in own]
        pivots = [[columns[j][k + i:k + i + 1, :] for j in own] for i in own]
        for q in own:
            turned = 1.0 / pivots[q][q]
            line = [turned if j == q else pivots[q][j] * turned for j in own]
            pivots = [
                line if i == q else [
                    -pivots[i][q] * turned if j == q else pivots[i][j] - pivots[i][q] * line[j] for j in own
                ] for i in own
            ]
        lines = []
        for i in own:
            line = value[k + i:k + i + 1, :]
            for j in own:
                line = jnp.where(over[:1] == k + j, 1.0 if i == j else 0.0, line)
            lines.append(line)
        lines = [sum(pivots[i][j] * lines[j] for j in own) for i in own]
        value = jnp.where((over >= k) & (over < k + block), 0.0, value)
        for j in own:
            value = value - columns[j] * lines[j]
        for j in own:
            value = jnp.where(down == k + j, lines[j], value)
    return value


def fused_kernel(n_grp, n_atm, *refs):
    small, refs = refs[:7], refs[7:]
    (p_hbm, p_ref, left_ref, right_ref, w_ref, *refs) = refs
    held, refs = refs[:7], refs[7:]
    (atoms_ref, kinds_ref, member_ref, targets_ref, weights_ref, bias_ref, readout_ref) = held
    (rows0, cols0, rows1, cols1, past_c, past_r,
     xt_ref, xa, aux, vec, hots, picks, slopes, jpart, jgot, jall, both, tacc, tpart, tgot, jpiece, gpiece, quarter, cplane, cz, wplane, wz,
     p_sem, x_sem, a_s, a_r, j_s, j_r, z_s, z_r, f_s, f_r, i_s, i_r, t_s, t_r, c_s, c_r, d_s, d_r, w_s, w_r, v_s, v_r,
     gr_s, gr_r, gz_s, gz_r, ga_s, ga_r, gf_s, gf_r) = refs
    rows_all, cols_all = (rows0, rows1), (cols0, cols1)
    row, col, z, core, plane, column, partner = places(n_grp, n_atm)
    n_z = n_grp // CORES
    seat = core * n_atm + col
    seats = CORES * n_atm
    others = [lax.rem(seat + d, seats) for d in range(1, seats)]
    floor = [{"grp": z * CORES + o // n_atm, "atm": lax.rem(o, n_atm)} for o in others]
    groups = GROUP_LOCAL * n_grp
    rows, width = p_ref.shape
    features, units = weights_ref.shape
    local = jpart.shape[1] - 1
    n_own = atoms_ref.shape[1]
    chunk = local // PARTS
    span = chunk * units
    piece = rows // n_atm
    per = piece // units
    deep = min(span, 2048)
    tall = min(piece, 512)
    steps = span // deep
    halves = [pl.ds(h * (groups // HALVES), groups // HALVES) for h in range(HALVES)]

    fetches = []
    for i, (source, target) in enumerate(zip(small, held)):
        fetch = pltpu.make_async_copy(source, target, x_sem.at[i])
        fetch.start()
        fetches.append(fetch)
    loads = []
    for k in range(PARTS):
        cut = pl.ds(k * span, span)
        load = pltpu.make_async_copy(p_hbm.at[:, cut], p_ref.at[:, cut], p_sem.at[k])
        load.start()
        loads.append(load)
    for fetch in fetches:
        fetch.wait()
    xt_ref[...] = atoms_ref[0].T
    xa[col] = atoms_ref[1]
    aux[col] = jnp.zeros((GROUP_LOCAL, n_own), jnp.float32)
    aux[col, :1] = kinds_ref[1:2, :].astype(jnp.float32)
    aux[col, 1:2] = member_ref[1:2, :].astype(jnp.float32)

    current = weights_ref[...]
    inverses, sends, bulk = [], [], {}
    iota8 = lax.broadcasted_iota(jnp.int32, (GROUP_LOCAL, units), 0)

    def gains_first(step, h, here):
        mine = quarter.at[step, z, halves[h]]
        quarter[step, z, halves[h]] = here
        far = [push(mine, mine, gz_s.at[step, h], gz_r.at[step, h], i, {"grp": p}) for i, p in enumerate(column)]
        bulk.setdefault((step, h), [[], []])[0] += far

    def gains_rows(step, h, here):
        place = rows_all[step].at[col, halves[h]]
        rows_all[step][col, halves[h]] = here
        bulk.setdefault((step, h), [[], []])[1] += [push(place, place, gr_s.at[step, h], gr_r.at[step, h], i, {"atm": p}) for i, p in enumerate(plane)]

    def gains_second(step, h):
        half = halves[h]
        for copy in bulk[step, h][0]:
            copy.wait_recv()
        out = cols_all[step]
        place = out.at[core, col, half]
        swap = [push(quarter.at[step, p, half], place, ga_s.at[step, h], ga_r.at[step, h], i, {"atm": p}) for i, p in enumerate(plane)]
        out[core, col, half] = quarter[step, col, half]
        last = [push(place, place, gf_s.at[step, h], gf_r.at[step, h], len(plane), {"grp": partner})]
        bulk[step, h] += [swap, last]

    def gains_third(step, h):
        out = cols_all[step]
        for i, copy in enumerate(bulk[step, h][2]):
            copy.wait_recv()
            origin = lax.rem(col + n_atm - (i + 1), n_atm)
            place = out.at[core, origin, halves[h]]
            bulk[step, h][3].append(push(place, place, gf_s.at[step, h], gf_r.at[step, h], i, {"grp": partner}))

    def gains_near(step):
        for h in range(HALVES):
            for copy in bulk[step, h][1]:
                copy.wait_recv()

    def gains_last(step):
        for h in range(HALVES):
            for copy in bulk[step, h][3]:
                copy.wait_recv()

    def typed(kinds_row):
        kinds_col = jnp.broadcast_to(kinds_row, (GROUP_LOCAL, n_own)).T[:, :1]
        vectors = jnp.zeros((n_own, units), jnp.float32)
        for kind in range(readout_ref.shape[0]):
            vectors = jnp.where(kinds_col == kind, readout_ref[kind:kind + 1, :], vectors)
        return vectors

    def grouped(member_row):
        return (lax.broadcasted_iota(jnp.int32, (GROUP_LOCAL, n_own), 0).astype(jnp.float32) == member_row).astype(jnp.float32)

    def picked(xs, hot):
        high = xs.astype(jnp.bfloat16).astype(jnp.float32)
        return [(v[:, None, :] * hot[None]).reshape(local * GROUP_LOCAL, n_own).astype(jnp.bfloat16) for v in (high, xs - high)]

    for step in range(STEPS):
        second, third = [], []
        cuts = [pl.ds(0, local + 1)]
        if step == 0:
            hidden = jnp.tanh(exact(atoms_ref[0], current) + bias_ref[...])
            vectors = typed(kinds_ref[:1, :].astype(jnp.float32))
            slope_high, slope_low = split((1.0 - hidden * hidden) * vectors)
            slope_both = jnp.concatenate([slope_high, slope_low], axis=1)
            hot = grouped(member_ref[:1, :].astype(jnp.float32))
            energy = exact(hot, hidden * vectors)
            energy = jnp.broadcast_to(jnp.sum(energy, axis=1, keepdims=True), (GROUP_LOCAL, units))

            def grads(p):
                high, low = picked(xt_ref[pl.ds(p * local, local), :], hot)
                one = jnp.dot(high, slope_both, preferred_element_type=jnp.float32)
                two = jnp.dot(low, slope_high, preferred_element_type=jnp.float32)
                total = one[:, :units] + one[:, units:] + two
                jpart[p, :local] = total.reshape(local, GROUP_LOCAL, units)
                jpart[p, local] = energy

            greet(floor + [{"grp": p} for p in column])
            first = []
            for i, p in enumerate(plane):
                grads(p)
                first.append(push(jpart.at[p], jgot.at[i], j_s, j_r, i, {"atm": p}))
            grads(col)
            total = jpart[col]
            for i, copy in enumerate(first):
                copy.wait_recv()
                total = total + jgot[i]
            jall[step, row] = total
            sends += first
        else:
            def slopes_of(s, energy):
                at = pl.ds(pl.multiple_of(s * n_own, n_own), n_own)
                hidden = jnp.tanh(exact(xa[s], current) + bias_ref[...])
                high, low = split((1.0 - hidden * hidden) * vec[s])
                slopes[at, :] = jnp.concatenate([high, low], axis=1)
                return energy + exact(hots[s], hidden * vec[s])

            energy = lax.fori_loop(0, n_atm, slopes_of, jnp.zeros((GROUP_LOCAL, units), jnp.float32))
            one = jnp.dot(picks[0], slopes[...], preferred_element_type=jnp.float32)
            two = jnp.dot(picks[1], slopes[:, :units], preferred_element_type=jnp.float32)
            total = one[:, :units] + one[:, units:] + two
            jall[step, row, :local] = total.reshape(local, GROUP_LOCAL, units)
            jall[step, row, local] = jnp.broadcast_to(jnp.sum(energy, axis=1, keepdims=True), (GROUP_LOCAL, units))

        place = jall.at[step, row]
        second.append([push(place, place, z_s.at[step], z_r.at[step], i, {"grp": p}) for i, p in enumerate(column)])
        third.append([push(place, place, f_s.at[step], f_r.at[step], len(column), {"grp": partner})])
        sends += second[0]
        if step == 0:
            gather = [push(xa.at[col], xa.at[col], a_s.at[0], a_r.at[0], i, {"atm": p}) for i, p in enumerate(plane)]
            gather += [push(aux.at[col], aux.at[col], a_s.at[1], a_r.at[1], i, {"atm": p}) for i, p in enumerate(plane)]
            sends += gather
            for copy in gather:
                copy.wait_recv()

            def prepare(s, carry):
                at = pl.ds(pl.multiple_of(s * n_own, n_own), n_own)
                hot = grouped(aux[s, 1:2])
                hots[s] = hot
                vec[s] = typed(aux[s, :1])
                xt_ref[...] = xa[s].T
                high, low = picked(xt_ref[pl.ds(col * local, local), :], hot)
                picks[0, :, at] = high
                picks[1, :, at] = low
                return carry
            lax.fori_loop(0, n_atm, prepare, 0)
        else:
            for h in range(HALVES):
                gains_rows(0, h, gpiece[0, halves[h]])
            for copy in early_sends:
                copy.wait_send()

        def forward(k):
            for i, copy in enumerate(second[k]):
                copy.wait_recv()
                origin = lax.rem(z + n_z - (i + 1), n_z) * CORES + core
                place = jall.at[step, origin]
                third[k].append(push(place, place, f_s.at[step], f_r.at[step], i, {"grp": partner}))

        def product(at, over):
            high, low = split(p_ref[pl.ds(at, tall), pl.ds(over, deep)])
            right = both[step, :, pl.ds(over, deep)]
            return across(high, right) + across(low, right)

        def some_rows(k, start, stop):
            def add(t, carry):
                at = pl.multiple_of(t // steps * tall, tall)
                over = pl.multiple_of(k * span + lax.rem(t, steps) * deep, deep)
                tacc[pl.ds(at, tall), :] += product(at, over)
                return carry
            lax.fori_loop(start * steps, stop * steps, add, 0)

        def last_rows(i, carry):
            p = lax.rem(col + 1 + i, n_atm)

            def add(t, carry):
                at = pl.multiple_of(p * piece + t // steps * tall, tall)
                over = pl.multiple_of((PARTS - 1) * span + lax.rem(t, steps) * deep, deep)
                tacc[pl.ds(at, tall), :] += product(at, over)
                return carry
            lax.fori_loop(0, piece // tall * steps, add, 0)
            value = tacc[pl.ds(pl.multiple_of(p * piece, piece), piece), :].T
            tpart[step, p] = value[:groups] + value[groups:]

            @pl.when(i < n_atm - 1)
            def _():
                for h in range(HALVES):
                    spread(h, i).start()
            return carry

        def spread(h, i):
            p = lax.rem(col + 1 + i, n_atm)
            return pltpu.make_async_remote_copy(
                src_ref=tpart.at[step, p, halves[h]], dst_ref=tgot.at[step, i, halves[h]],
                send_sem=t_s.at[step, h, i], recv_sem=t_r.at[step, h, i], device_id={"atm": p}, device_id_type=MESH)

        tacc[...] = jnp.zeros_like(tacc)
        scatter = [[spread(h, i) for i in range(n_atm - 1)] for h in range(HALVES)]
        forward(0)
        if step == 1:
            for h in range(HALVES):
                gains_first(0, h, gpiece[0, halves[h]])
        for k in range(PARTS):
            for copy in third[k]:
                copy.wait_recv()
            sends += third[k]
            for i in range(k * chunk, (k + 1) * chunk):
                high, low = split(jall[step, :, i].reshape(groups, units))
                both[step, :groups, i * units:(i + 1) * units] = high
                both[step, groups:, i * units:(i + 1) * units] = low
            if step == 0:
                loads[k].wait()
            if k < PARTS - 1:
                some_rows(k, 0, rows // tall // 2)
                forward(k + 1)
                some_rows(k, rows // tall // 2, rows // tall)
            else:
                inner = local // CORES
                window = lambda p: pl.ds(core * inner + p * per, per)
                jp_copies = [pltpu.make_async_remote_copy(
                    src_ref=jall.at[step, :, window(p)], dst_ref=jpiece.at[step], send_sem=i_s.at[step, i], recv_sem=i_r.at[step],
                    device_id={"atm": p}, device_id_type=MESH) for i, p in enumerate(plane)]

                @pl.when(col == z)
                def _():
                    for copy in jp_copies:
                        copy.start()
                    jpiece[step] = jall[step, :, window(col)]

                lax.fori_loop(0, n_atm, last_rows, 0)
        for h, half in enumerate(halves):
            sends += scatter[h]
            gain = tpart[step, col, half]
            for i, copy in enumerate(scatter[h]):
                copy.wait_recv()
                gain = gain + tgot[step, i, half]
            gpiece[step, half] = gain
            if step == STEPS - 1:
                gains_first(step, h, gain)
                gains_rows(step, h, gain)
        gain = gpiece[step]

        @pl.when(col != z)
        def _():
            jp_copies[0].wait_recv()

        @pl.when(col == z)
        def _():
            for copy in jp_copies:
                copy.wait_send()

        jp = jnp.concatenate([jpiece[step, :, j].reshape(groups, units) for j in range(per)], axis=1)
        stack = gain if step == 0 else jnp.concatenate([gain] + [gpiece[s] for s in range(step)], axis=0)
        terms = across(jp, stack, precision=precise)
        if step == 0:
            terms = jnp.concatenate([terms[:groups // 2], terms[groups // 2:]], axis=1)
        size = pl.ds(0, terms.shape[0])
        cplane[step, seat, size] = terms
        place = cplane.at[step, seat, size]
        hop = [push(place, place, c_s.at[step], c_r.at[step], i, d) for i, d in enumerate(floor)]
        for copy in hop:
            copy.wait_recv()
        if step == 1:
            for h in range(HALVES):
                gains_second(0, h)
        terms = cplane[step, 0, size]
        for i in range(1, seats):
            terms = terms + cplane[step, i, size]
        cz[step, z, size] = terms
        place = cz.at[step, z, size]
        skip = [push(place, place, d_s.at[step], d_r.at[step], i, {"grp": p}) for i, p in enumerate(column)]
        for copy in skip:
            copy.wait_recv()
        sends += hop + skip
        terms = cz[step, 0, size]
        for i in range(1, n_z):
            terms = terms + cz[step, i, size]
        if step == 0:
            curve = jnp.concatenate([terms[:, :groups], terms[:, groups:]], axis=0)
        else:
            cross = terms[:, groups:]
            early = exact(cross, inverses[0])
            curve = (terms[:, :groups] - across(early, cross, precision=precise)) * (1.0 / forget_rate)
        down = lax.broadcasted_iota(jnp.int32, (groups, groups), 0)
        over = lax.broadcasted_iota(jnp.int32, (groups, groups), 1)
        inverse = 0.5 * (curve + curve.T) + jnp.where(down == over, forget_rate, 0.0)
        inverse = spd_sweep(inverse, 0, groups // 2)
        if step == 1:
            for h in range(HALVES):
                gains_third(0, h)
            gains_second(step, 0)
        inverse = spd_sweep(inverse, groups // 2, groups)
        if step == 1:
            for h in range(1, HALVES):
                gains_second(step, h)
        inverses.append(inverse)
        if step == 1:
            gain = (gain - exact(early, gpiece[0])) * (1.0 / forget_rate)

        predicted = jall[step, :, local].reshape(groups, units).T
        mismatch = jnp.broadcast_to(targets_ref[step:step + 1, :], (GROUP_LOCAL, groups)) - predicted[:GROUP_LOCAL]
        change = exact(exact(mismatch, inverse), gain)
        turn = lax.rem(iota8, per)
        mine = change[:, :units]
        for j in range(1, per):
            mine = jnp.where(turn == j, change[:, j * units:(j + 1) * units], mine)
        wplane[step, seat] = mine
        place = wplane.at[step, seat]
        hop = [push(place, place, w_s.at[step], w_r.at[step], i, d) for i, d in enumerate(floor)]
        if step == 1:
            gains_third(step, 0)
        for copy in hop:
            copy.wait_recv()
        fold = GROUP_LOCAL // per
        for m in range(seats // fold):
            dense = wplane[step, m * fold]
            for j in range(1, fold):
                dense = jnp.where(iota8 >= j * per, wplane[step, m * fold + j], dense)
            wz[step, z, m * GROUP_LOCAL:(m + 1) * GROUP_LOCAL] = dense
        place = wz.at[step, z]
        skip = [push(place, place, v_s.at[step], v_r.at[step], i, {"grp": p}) for i, p in enumerate(column)]
        sends += hop + skip
        if step == 1:
            for h in range(1, HALVES):
                gains_third(step, h)
            gains_near(0)
            gains_last(0)
            scaled = inverses[0] * (1.0 / forget_rate ** STEPS)
            for b in range(seats):
                high, low = split(triple(scaled, cols0[b // n_atm, b % n_atm]))
                right_ref[:groups, b * piece:(b + 1) * piece] = high
                right_ref[STEPS * groups:(STEPS + 1) * groups, b * piece:(b + 1) * piece] = low
            past = early * (1.0 / forget_rate)
            for b in range(seats):
                past_c[b] = triple(past, cols0[b // n_atm, b % n_atm])
            gains_near(1)
            for p in range(n_atm):
                later = rows1[p] * (1.0 / forget_rate) - triple(past, rows0[p])
                high, low = split(jnp.concatenate([rows0[p], later], axis=0).T)
                left_ref[p * piece:(p + 1) * piece, :] = jnp.concatenate([high, low], axis=1)
        for copy in skip:
            copy.wait_recv()
        current = current + wz[step].reshape(features, units)
        if step == 0:
            early_sends, sends = sends, []

    w_ref[...] = current
    for part in bulk.values():
        sends += sum(part[:3], [])
    for copy in sends:
        copy.wait_send()
    gains_last(1)
    scaled = inverses[1] * (1.0 / forget_rate)
    for b in range(seats):
        later = cols1[b // n_atm, b % n_atm] * (1.0 / forget_rate) - past_c[b]
        high, low = split(triple(scaled, later))
        right_ref[groups:STEPS * groups, b * piece:(b + 1) * piece] = high
        right_ref[(STEPS + 1) * groups:, b * piece:(b + 1) * piece] = low
    for part in bulk.values():
        for copy in part[3]:
            copy.wait_send()


def fused(*args, n_grp, n_atm):
    atoms, kinds, member, targets, weights, bias, readout, covariance = args
    small = [atoms, kinds, member, targets, weights, bias.reshape(1, -1), readout]
    rows, width = covariance.shape
    units = weights.shape[1]
    groups = GROUP_LOCAL * n_grp
    n_z = n_grp // CORES
    seats = CORES * n_atm
    local = width // units
    piece = rows // n_atm
    per = piece // units
    n_own = atoms.shape[1]
    block = (local + 1, GROUP_LOCAL, units)
    f32 = jnp.float32
    dma = pltpu.SemaphoreType.DMA
    vm = lambda *shape: pltpu.VMEM(shape, f32)
    pair = lambda *shape: [dma((STEPS,) + shape)] * 2
    out_shape = (
        vm(rows, width),
        jax.ShapeDtypeStruct((rows, 2 * STEPS * groups), jnp.bfloat16),
        jax.ShapeDtypeStruct((2 * STEPS * groups, width), jnp.bfloat16),
        jax.ShapeDtypeStruct(weights.shape, f32),
    )
    HBM = pl.BlockSpec(memory_space=pltpu.HBM)
    covar, *outs = pl.pallas_call(
        functools.partial(fused_kernel, n_grp, n_atm),
        out_shape=out_shape,
        in_specs=[HBM] * 8,
        out_specs=(VM,) * len(out_shape),
        scratch_shapes=[pltpu.VMEM(v.shape, v.dtype) for v in small]
        + [vm(n_atm, groups, piece), vm(CORES, n_atm, groups, piece)] * 2
        + [
            vm(seats, groups, piece), vm(n_atm, groups, piece),
            vm(atoms.shape[2], n_own),
            vm(n_atm, n_own, atoms.shape[2]), vm(n_atm, GROUP_LOCAL, n_own), vm(n_atm, n_own, units), vm(n_atm, GROUP_LOCAL, n_own),
            pltpu.VMEM((2, local * GROUP_LOCAL, n_atm * n_own), jnp.bfloat16), pltpu.VMEM((n_atm * n_own, 2 * units), jnp.bfloat16),
            vm(n_atm, *block), vm(n_atm - 1, *block), vm(STEPS, n_grp, *block),
            pltpu.VMEM((STEPS, 2 * groups, width), jnp.bfloat16),
            vm(rows, 2 * groups),
            vm(STEPS, n_atm, groups, piece), vm(STEPS, n_atm - 1, groups, piece),
            vm(STEPS, n_grp, per, GROUP_LOCAL, units), vm(STEPS, groups, piece), vm(STEPS, n_z, groups, piece),
            vm(STEPS, seats, groups, STEPS * groups), vm(STEPS, n_z, groups, STEPS * groups),
            vm(STEPS, seats, GROUP_LOCAL, units), vm(STEPS, n_z, seats * per, units),
            dma((PARTS,)), dma((len(small),)),
        ] + [dma((2, n_atm - 1))] * 2 + [dma((n_atm - 1,))] * 2 + pair(n_z - 1) + pair(n_z)
        + [dma((STEPS, n_atm - 1)), dma((STEPS,))] + pair(HALVES, n_atm - 1)
        + pair(seats - 1) + pair(n_z - 1) + pair(seats - 1) + pair(n_z - 1)
        + pair(HALVES, n_atm - 1) + pair(HALVES, n_z - 1) + pair(HALVES, n_atm - 1) + pair(HALVES, n_atm),
        compiler_params=pltpu.CompilerParams(collective_id=4, has_side_effects=True, vmem_limit_bytes=30 << 20),
        name="updates",
    )(*small, covariance)
    return [pltpu.with_memory_space_constraint(covar, pltpu.VMEM), *outs]


def finish_kernel(tile, p_ref, left_ref, right_ref, w_in, out_ref, w_out, ring, sem):
    w_out[...] = w_in[...]
    rows, width = p_ref.shape
    depth = left_ref.shape[1] // 2
    part = min(width, 512)

    def leave(t):
        slot = lax.rem(t, RING)
        return pltpu.make_async_copy(ring.at[slot], out_ref.at[pl.ds(pl.multiple_of(t * tile, tile), tile)], sem.at[slot])

    def one(t, carry):
        @pl.when(t >= RING)
        def _():
            leave(t - RING).wait()

        here = pl.ds(pl.multiple_of(t * tile, tile), tile)
        slot = lax.rem(t, RING)
        high, low = left_ref[here, :depth], left_ref[here, depth:]
        twice = jnp.concatenate([high, high], axis=1)
        for k in range(0, width, part):
            cut = slice(k, k + part)
            down = jnp.dot(twice, right_ref[:, cut], preferred_element_type=jnp.float32)
            down = down + jnp.dot(low, right_ref[:depth, cut], preferred_element_type=jnp.float32)
            ring[slot, :, cut] = p_ref[here, cut] * (1.0 / forget_rate ** STEPS) - down
        leave(t).start()
        return carry

    lax.fori_loop(0, rows // tile, one, 0)
    for t in range(rows // tile - RING, rows // tile):
        leave(t).wait()


def finish(covar, left, right, weights):
    rows, width = covar.shape
    tile = min(rows // RING, 128)
    return pl.pallas_call(
        functools.partial(finish_kernel, tile),
        out_shape=(jax.ShapeDtypeStruct((rows, width), jnp.float32), jax.ShapeDtypeStruct(weights.shape, jnp.float32)),
        in_specs=[VM] * 4,
        out_specs=(pl.BlockSpec(memory_space=pltpu.HBM), VM),
        scratch_shapes=[pltpu.VMEM((RING, tile, width), jnp.float32), pltpu.SemaphoreType.DMA((RING,))],
        compiler_params=pltpu.CompilerParams(vmem_limit_bytes=30 << 20),
        name="finish",
    )(covar, left, right, weights)


def terms_kernel(groups, jac_ref, p_ref, out_ref, both):
    @pl.when(pl.program_id(0) == 0)
    def _():
        jac = jac_ref[...]
        high = jac.astype(jnp.bfloat16).astype(jnp.float32)
        both[...] = jnp.concatenate([high, jac - high], axis=0).T.astype(jnp.bfloat16)

    high, low = split(p_ref[...])
    one = jnp.dot(high, both[...], preferred_element_type=jnp.float32)
    two = jnp.dot(low, both[...], preferred_element_type=jnp.float32)
    one = one.T
    out_ref[0] = one[:groups] + one[groups:] + two.T[:groups]


def row_terms(covar, jac, n_atm):
    rows, width = covar.shape
    groups = jac.shape[0]
    piece = rows // n_atm
    tile = min(piece, 256)
    per = piece // tile
    return pl.pallas_call(
        functools.partial(terms_kernel, groups),
        grid=(rows // tile,),
        out_shape=jax.ShapeDtypeStruct((n_atm, groups, piece), jnp.float32),
        in_specs=[
            pl.BlockSpec((groups, width), lambda i: (0, 0)),
            pl.BlockSpec((tile, width), lambda i: (i, 0)),
        ],
        out_specs=pl.BlockSpec((1, groups, tile), lambda i: (i // per, 0, lax.rem(i, per))),
        scratch_shapes=[pltpu.VMEM((width, 2 * groups), jnp.bfloat16)],
        compiler_params=pltpu.CompilerParams(vmem_limit_bytes=48 << 20),
        name="row_terms",
    )(jac, covar)


def update_kernel(scale, left_ref, right_ref, p_ref, out_ref, right):
    @pl.when(pl.program_id(0) == 0)
    def _():
        high, low = split(right_ref[...])
        right[...] = jnp.concatenate([high, high, low], axis=0)

    high, low = split(left_ref[...])
    left = jnp.concatenate([high, low, high], axis=1)
    width = p_ref.shape[1]
    part = min(width, 512)
    for k in range(0, width, part):
        down = jnp.dot(left, right[:, k:k + part], preferred_element_type=jnp.float32)
        out_ref[:, k:k + part] = p_ref[:, k:k + part] * scale - down


def final_update(covar, left, right):
    rows, width = covar.shape
    depth = left.shape[1]
    tile = min(rows, 256)
    return pl.pallas_call(
        functools.partial(update_kernel, 1.0 / forget_rate ** STEPS),
        grid=(rows // tile,),
        out_shape=jax.ShapeDtypeStruct((rows, width), jnp.float32),
        in_specs=[
            pl.BlockSpec((tile, depth), lambda i: (i, 0)),
            pl.BlockSpec((depth, width), lambda i: (0, 0)),
            pl.BlockSpec((tile, width), lambda i: (i, 0)),
        ],
        out_specs=pl.BlockSpec((tile, width), lambda i: (i, 0)),
        scratch_shapes=[pltpu.VMEM((3 * depth, width), jnp.bfloat16)],
        compiler_params=pltpu.CompilerParams(vmem_limit_bytes=48 << 20),
        name="final_update",
    )(left, right, covar)


def body(atoms, kinds, member, targets, weights, bias, readout, covariance):
    n_grp, n_atm = lax.axis_size("grp"), lax.axis_size("atm")
    rows, width = covariance.shape
    units = weights.shape[1]
    if n_grp == CORES * n_atm and rows % (n_atm * units) == 0 and GROUP_LOCAL % (rows // (n_atm * units)) == 0:
        return finish(*fused(
            atoms, kinds, member, targets, weights, bias, readout, covariance, n_grp=n_grp, n_atm=n_atm
        ))
    groups = GROUP_LOCAL * n_grp
    dot = functools.partial(jnp.dot, precision=precise)
    current = weights
    past = []
    for step in range(STEPS):
        energies, partial_value = local_terms(
            atoms[step], kinds[step], member[step], current, bias, readout
        )
        blocks = partial_value.reshape(GROUP_LOCAL, n_atm, width).transpose(1, 0, 2)
        tail = jnp.broadcast_to(energies[None, :, None], (n_atm, GROUP_LOCAL, LANES))
        shared = share_grads(jnp.concatenate([blocks, tail], axis=2), n_grp, n_atm)
        shared = shared.reshape(groups, width + LANES)
        jac = shared[:, :width]
        mismatch = targets[step] - shared[:, width]
        terms = row_terms(covariance, jac, n_atm) * (1.0 / forget_rate ** step)
        for age, (rows_old, cols_old, inverse_old) in enumerate(past):
            small = lax.dot_general(jac, cols_old, (((1,), (1,)), ((), ())), precision=precise)
            small = dot(small, inverse_old) * (1.0 / forget_rate ** (step - age))
            terms = terms - jnp.einsum("xy,nyp->nxp", small, rows_old, precision=precise)
        rows, cols = share_gains(terms, n_grp, n_atm)
        part = lax.dot_general(jac, cols, (((1,), (1,)), ((), ())), precision=precise)
        inverse = innovation_inverse(gather_atm(part, n_atm, 2))
        coefficient = dot(inverse, mismatch)
        change = dot(coefficient, cols).reshape(-1, current.shape[1])
        current = current + gather_atm(change, n_atm, 3).reshape(current.shape)
        past.append((rows, cols, inverse))
    left, right = [], []
    for age, (rows, cols, inverse) in enumerate(past):
        scaled = jnp.einsum("nxp,xy->npy", rows, inverse, precision=precise)
        left.append(scaled.reshape(-1, groups) * (1.0 / forget_rate ** (STEPS - age)))
        right.append(cols)
    covar = final_update(covariance, jnp.concatenate(left, axis=1), jnp.concatenate(right, axis=0))
    return (covar, current)


def solution(mesh):
    return jax.shard_map(
        body,
        mesh=mesh,
        in_specs=(
            P(None, ("grp", "atm"), None),
            P(None, ("grp", "atm")),
            P(None, ("grp", "atm")),
            P(),
            P(),
            P(),
            P(),
            P("grp", "atm"),
        ),
        out_specs=(P("grp", "atm"), P()),
        check_vma=False,
    )
```

```python
import functools
import jax
import jax.numpy as jnp
from jax import lax
from jax.experimental import pallas as pl
from jax.experimental.pallas import tpu as pltpu
from jax.sharding import PartitionSpec as P

GROUP_LOCAL = 8
STEPS = 2
CORES = 2
LANES = 128
CHUNKS = 2
PARTS = 1
HALVES = 1
RING = 3

forget_rate = 0.98
precise = lax.Precision.HIGHEST
MESH = pl.DeviceIdType.MESH
VM = pl.BlockSpec(memory_space=pltpu.VMEM)


def local_terms(atoms, kinds, member, weights, bias, readout):
    preact = jnp.dot(atoms, weights, precision=precise, preferred_element_type=jnp.float32) + bias
    hidden = jnp.tanh(preact)
    type_hot = (kinds[:, None] == jnp.arange(readout.shape[0])[None, :]).astype(jnp.float32)
    vectors = jnp.dot(type_hot, readout, precision=precise)
    atom_energy = jnp.sum(hidden * vectors, axis=1)
    slope = (1.0 - hidden * hidden) * vectors
    group_hot = (member[:, None] == jnp.arange(GROUP_LOCAL)[None, :]).astype(jnp.float32)
    energies = jnp.dot(atom_energy, group_hot, precision=precise)
    masked = atoms[:, None, :] * group_hot[:, :, None]
    grads = jnp.einsum("agi,ac->gic", masked, slope, precision=precise)
    return energies, grads.reshape(GROUP_LOCAL, -1)


def push(src, dst, sems, recvs, slot, target):
    copy = pltpu.make_async_remote_copy(
        src_ref=src, dst_ref=dst, send_sem=sems.at[slot], recv_sem=recvs.at[slot],
        device_id=target, device_id_type=MESH,
    )
    copy.start()
    return copy


def greet(targets):
    barrier = pltpu.get_barrier_semaphore()
    for target in targets:
        pl.semaphore_signal(barrier, inc=1, device_id=target, device_id_type=MESH)
    pl.semaphore_wait(barrier, len(targets))


def places(n_grp, n_atm):
    row, col = lax.axis_index("grp"), lax.axis_index("atm")
    n_z = n_grp // CORES
    z, core = row // CORES, lax.rem(row, CORES)
    plane = [lax.rem(col + d, n_atm) for d in range(1, n_atm)]
    column = [lax.rem(z + d, n_z) * CORES + core for d in range(1, n_z)]
    partner = z * CORES + (CORES - 1 - core)
    return row, col, z, core, plane, column, partner


def grads_kernel(n_grp, n_atm, x_ref, out_ref, got, a_s, a_r, b_s, b_r, f_s, f_r):
    row, col, z, core, plane, column, partner = places(n_grp, n_atm)
    greet([{"atm": p} for p in plane] + [{"grp": p} for p in column] + [{"grp": partner}])
    n_z = n_grp // CORES
    wide = x_ref.shape[2]
    middle = wide // 2 // LANES * LANES
    cuts = [pl.ds(0, middle), pl.ds(middle, wide - middle)]
    first, second, last = [], [], []
    for k, cut in enumerate(cuts):
        first.append([push(x_ref.at[p, :, cut], got.at[i, :, cut], a_s.at[k], a_r.at[k], i, {"atm": p}) for i, p in enumerate(plane)])
    for k, cut in enumerate(cuts):
        total = x_ref[col, :, cut]
        for i, copy in enumerate(first[k]):
            copy.wait_recv()
            total = total + got[i, :, cut]
        out_ref[row, :, cut] = total
        place = out_ref.at[row, :, cut]
        second.append([push(place, place, b_s.at[k], b_r.at[k], i, {"grp": p}) for i, p in enumerate(column)])
        last.append(push(place, place, f_s.at[k], f_r.at[k], len(column), {"grp": partner}))
    for k, cut in enumerate(cuts):
        for i, copy in enumerate(second[k]):
            copy.wait_recv()
            origin = lax.rem(z + n_z - (i + 1), n_z) * CORES + core
            place = out_ref.at[origin, :, cut]
            last.append(push(place, place, f_s.at[k], f_r.at[k], i, {"grp": partner}))
    for copy in last:
        copy.wait_recv()
    for copy in sum(first + second, last):
        copy.wait_send()


def share_grads(x, n_grp, n_atm):
    block = x.shape[1:]
    n_z = n_grp // CORES
    dma = pltpu.SemaphoreType.DMA
    return pl.pallas_call(
        functools.partial(grads_kernel, n_grp, n_atm),
        out_shape=jax.ShapeDtypeStruct((n_grp,) + block, jnp.float32),
        in_specs=[VM], out_specs=VM,
        scratch_shapes=[pltpu.VMEM((n_atm - 1,) + block, jnp.float32)]
        + [dma((2, n_atm - 1))] * 2 + [dma((2, n_z - 1))] * 2 + [dma((2, n_z))] * 2,
        compiler_params=pltpu.CompilerParams(collective_id=0, has_side_effects=True),
        name="share_grads",
    )(x)


def gains_kernel(n_grp, n_atm, half, t_ref, row_ref, col_ref, got, quarter,
                 a_s, a_r, r_s, r_r, b_s, b_r, c_s, c_r, f_s, f_r):
    row, col, z, core, plane, column, partner = places(n_grp, n_atm)
    greet([{"atm": p} for p in plane] + [{"grp": p} for p in column] + [{"grp": partner}])
    groups = t_ref.shape[1]
    chunk = groups // CHUNKS
    cuts = [pl.ds(k * chunk, chunk) for k in range(CHUNKS)]
    first, along, rows, across, last = [], [], [], [], []
    for k, cut in enumerate(cuts):
        first.append([push(t_ref.at[p, cut], got.at[i, cut], a_s.at[k], a_r.at[k], i, {"atm": p}) for i, p in enumerate(plane)])
    for k, cut in enumerate(cuts):
        total = t_ref[col, cut]
        for i, copy in enumerate(first[k]):
            copy.wait_recv()
            total = total + got[i, cut]
        quarter[z, cut] = total
        row_ref[col, cut] = total
        along.append([push(quarter.at[z, cut], quarter.at[z, cut], b_s.at[k], b_r.at[k], i, {"grp": p}) for i, p in enumerate(column)])
        rows.append([push(row_ref.at[col, cut], row_ref.at[col, cut], r_s.at[k], r_r.at[k], i, {"atm": p}) for i, p in enumerate(plane)])
    for k, cut in enumerate(cuts):
        for copy in along[k]:
            copy.wait_recv()
        across.append([
            push(quarter.at[pl.ds(p * half, half), cut], col_ref.at[core, col, :, cut], c_s.at[k], c_r.at[k], i, {"atm": p})
            for i, p in enumerate(plane)
        ])
        col_ref[core, col, :, cut] = quarter[pl.ds(col * half, half), cut]
        place = col_ref.at[core, col, :, cut]
        last.append([push(place, place, f_s.at[k], f_r.at[k], len(plane), {"grp": partner})])
    for k, cut in enumerate(cuts):
        for i, copy in enumerate(across[k]):
            copy.wait_recv()
            origin = lax.rem(col + n_atm - (i + 1), n_atm)
            place = col_ref.at[core, origin, :, cut]
            last[k].append(push(place, place, f_s.at[k], f_r.at[k], i, {"grp": partner}))
    for group in rows + last:
        for copy in group:
            copy.wait_recv()
    for group in first + along + rows + across + last:
        for copy in group:
            copy.wait_send()


def share_gains(t, n_grp, n_atm):
    _, groups, piece = t.shape
    per_col = n_grp // n_atm
    if n_grp % n_atm or per_col % CORES:
        mine = lax.psum(t, "atm")
        full = lax.all_gather(mine, "grp", axis=0).transpose(2, 0, 1, 3).reshape(groups, -1)
        width = full.shape[1] // n_atm
        return mine, lax.dynamic_slice_in_dim(full, lax.axis_index("atm") * width, width, 1)
    half = per_col // CORES
    n_z = n_grp // CORES
    dma = pltpu.SemaphoreType.DMA
    vm = lambda *lead: pltpu.VMEM(lead + (groups, piece), jnp.float32)
    rows, cols = pl.pallas_call(
        functools.partial(gains_kernel, n_grp, n_atm, half),
        out_shape=(
            jax.ShapeDtypeStruct((n_atm, groups, piece), jnp.float32),
            jax.ShapeDtypeStruct((CORES, n_atm, half, groups, piece), jnp.float32),
        ),
        in_specs=[VM], out_specs=(VM, VM),
        scratch_shapes=[vm(n_atm - 1), vm(n_z)]
        + [dma((CHUNKS, n_atm - 1))] * 4 + [dma((CHUNKS, n_z - 1))] * 2 + [dma((CHUNKS, n_atm - 1))] * 2 + [dma((CHUNKS, n_atm))] * 2,
        compiler_params=pltpu.CompilerParams(collective_id=1, has_side_effects=True),
        name="share_gains",
    )(t)
    return rows, cols.transpose(3, 2, 0, 1, 4).reshape(groups, -1)


def gather_kernel(n_atm, v_ref, out_ref, s, r):
    col = lax.axis_index("atm")
    plane = [lax.rem(col + d, n_atm) for d in range(1, n_atm)]
    greet([{"atm": p} for p in plane])
    copies = [push(v_ref, out_ref.at[col], s, r, i, {"atm": p}) for i, p in enumerate(plane)]
    out_ref[col] = v_ref[...]
    for copy in copies:
        copy.wait()


def gather_atm(v, n_atm, ident):
    return pl.pallas_call(
        functools.partial(gather_kernel, n_atm),
        out_shape=jax.ShapeDtypeStruct((n_atm,) + v.shape, jnp.float32),
        in_specs=[VM], out_specs=VM,
        scratch_shapes=[pltpu.SemaphoreType.DMA((n_atm - 1,))] * 2,
        compiler_params=pltpu.CompilerParams(collective_id=ident, has_side_effects=True),
        name="gather_atm%d" % ident,
    )(v)


def inverse_kernel(parts_ref, out_ref, work):
    size = out_ref.shape[0]
    total = parts_ref[0]
    for k in range(1, parts_ref.shape[0]):
        total = total + parts_ref[k]
    down = lax.broadcasted_iota(jnp.int32, (size, size), 0)
    over = lax.broadcasted_iota(jnp.int32, (size, size), 1)
    work[...] = 0.5 * (total + total.T) + jnp.where(down == over, forget_rate, 0.0)

    def sweep(k, carry):
        full = work[...]
        row = work[pl.ds(k, 1), :]
        column = jnp.sum(jnp.where(over == k, full, 0.0), axis=1, keepdims=True)
        pivot = 1.0 / jnp.sum(jnp.where(over[:1] == k, row, 0.0), axis=1, keepdims=True)
        row_part, col_part = row * pivot, column * pivot
        swept = full - column * row_part
        swept = jnp.where(down == k, row_part, swept)
        swept = jnp.where(over == k, col_part, swept)
        work[...] = jnp.where((down == k) & (over == k), -pivot, swept)
        return carry

    lax.fori_loop(0, size, sweep, 0)
    out_ref[...] = -work[...]


def innovation_inverse(parts):
    size = parts.shape[-1]
    return pl.pallas_call(
        inverse_kernel,
        out_shape=jax.ShapeDtypeStruct((size, size), jnp.float32),
        in_specs=[VM], out_specs=VM,
        scratch_shapes=[pltpu.VMEM((size, size), jnp.float32)],
        name="innovation_inverse",
    )(parts)


def split(value):
    high = value.astype(jnp.bfloat16)
    return high, (value - high.astype(jnp.float32)).astype(jnp.bfloat16)


def across(a, b, **options):
    return lax.dot_general(a, b, (((1,), (1,)), ((), ())), preferred_element_type=jnp.float32, **options)


def exact(a, b):
    return jnp.dot(a, b, precision=precise, preferred_element_type=jnp.float32)


def triple(a, b):
    high, low = split(a)
    high_b, low_b = split(b)
    left = jnp.concatenate([high, low, high], axis=1)
    right = jnp.concatenate([high_b, high_b, low_b], axis=0)
    return jnp.dot(left, right, preferred_element_type=jnp.float32)


def spd_sweep(value, start, stop, block=4):
    size = value.shape[0]
    down = lax.broadcasted_iota(jnp.int32, (size, size), 0)
    over = lax.broadcasted_iota(jnp.int32, (size, size), 1)
    for k in range(start, stop, block):
        own = range(block)
        columns = [jnp.broadcast_to(value[:, k + j:k + j + 1], (size, size)) for j in own]
        pivots = [[columns[j][k + i:k + i + 1, :] for j in own] for i in own]
        for q in own:
            turned = 1.0 / pivots[q][q]
            line = [turned if j == q else pivots[q][j] * turned for j in own]
            pivots = [
                line if i == q else [
                    -pivots[i][q] * turned if j == q else pivots[i][j] - pivots[i][q] * line[j] for j in own
                ] for i in own
            ]
        lines = []
        for i in own:
            line = value[k + i:k + i + 1, :]
            for j in own:
                line = jnp.where(over[:1] == k + j, 1.0 if i == j else 0.0, line)
            lines.append(line)
        lines = [sum(pivots[i][j] * lines[j] for j in own) for i in own]
        value = jnp.where((over >= k) & (over < k + block), 0.0, value)
        for j in own:
            value = value - columns[j] * lines[j]
        for j in own:
            value = jnp.where(down == k + j, lines[j], value)
    return value


def fused_kernel(n_grp, n_atm, *refs):
    small, refs = refs[:7], refs[7:]
    (p_hbm, p_ref, left_ref, right_ref, w_ref, *refs) = refs
    held, refs = refs[:7], refs[7:]
    (atoms_ref, kinds_ref, member_ref, targets_ref, weights_ref, bias_ref, readout_ref) = held
    (rows0, cols0, rows1, cols1, past_c, past_r,
     xt_ref, xa, aux, vec, hots, picks, slopes, jpart, jgot, jall, both, tacc, tpart, tgot, jpiece, gpiece, quarter, cplane, cz, wplane, wz,
     p_sem, x_sem, a_s, a_r, j_s, j_r, z_s, z_r, f_s, f_r, i_s, i_r, t_s, t_r, c_s, c_r, d_s, d_r, w_s, w_r, v_s, v_r,
     gr_s, gr_r, gz_s, gz_r, ga_s, ga_r, gf_s, gf_r) = refs
    rows_all, cols_all = (rows0, rows1), (cols0, cols1)
    row, col, z, core, plane, column, partner = places(n_grp, n_atm)
    n_z = n_grp // CORES
    seat = core * n_atm + col
    seats = CORES * n_atm
    others = [lax.rem(seat + d, seats) for d in range(1, seats)]
    floor = [{"grp": z * CORES + o // n_atm, "atm": lax.rem(o, n_atm)} for o in others]
    groups = GROUP_LOCAL * n_grp
    rows, width = p_ref.shape
    features, units = weights_ref.shape
    local = jpart.shape[1] - 1
    n_own = atoms_ref.shape[1]
    chunk = local // PARTS
    span = chunk * units
    piece = rows // n_atm
    per = piece // units
    deep = min(span, 2048)
    tall = min(piece, 512)
    steps = span // deep
    halves = [pl.ds(h * (groups // HALVES), groups // HALVES) for h in range(HALVES)]

    fetches = []
    for i, (source, target) in enumerate(zip(small, held)):
        fetch = pltpu.make_async_copy(source, target, x_sem.at[i])
        fetch.start()
        fetches.append(fetch)
    loads = []
    for k in range(PARTS):
        cut = pl.ds(k * span, span)
        load = pltpu.make_async_copy(p_hbm.at[:, cut], p_ref.at[:, cut], p_sem.at[k])
        load.start()
        loads.append(load)
    for fetch in fetches:
        fetch.wait()
    xt_ref[...] = atoms_ref[0].T
    xa[col] = atoms_ref[1]
    aux[col] = jnp.zeros((GROUP_LOCAL, n_own), jnp.float32)
    aux[col, :1] = kinds_ref[1:2, :].astype(jnp.float32)
    aux[col, 1:2] = member_ref[1:2, :].astype(jnp.float32)

    current = weights_ref[...]
    inverses, sends, bulk = [], [], {}
    iota8 = lax.broadcasted_iota(jnp.int32, (GROUP_LOCAL, units), 0)

    def gains_first(step, h, here):
        mine = quarter.at[step, z, halves[h]]
        quarter[step, z, halves[h]] = here
        far = [push(mine, mine, gz_s.at[step, h], gz_r.at[step, h], i, {"grp": p}) for i, p in enumerate(column)]
        bulk.setdefault((step, h), [[], []])[0] += far

    def gains_rows(step, h, here):
        place = rows_all[step].at[col, halves[h]]
        rows_all[step][col, halves[h]] = here
        bulk.setdefault((step, h), [[], []])[1] += [push(place, place, gr_s.at[step, h], gr_r.at[step, h], i, {"atm": p}) for i, p in enumerate(plane)]

    def gains_second(step, h):
        half = halves[h]
        for copy in bulk[step, h][0]:
            copy.wait_recv()
        out = cols_all[step]
        place = out.at[core, col, half]
        swap = [push(quarter.at[step, p, half], place, ga_s.at[step, h], ga_r.at[step, h], i, {"atm": p}) for i, p in enumerate(plane)]
        out[core, col, half] = quarter[step, col, half]
        last = [push(place, place, gf_s.at[step, h], gf_r.at[step, h], len(plane), {"grp": partner})]
        bulk[step, h] += [swap, last]

    def gains_third(step, h):
        out = cols_all[step]
        for i, copy in enumerate(bulk[step, h][2]):
            copy.wait_recv()
            origin = lax.rem(col + n_atm - (i + 1), n_atm)
            place = out.at[core, origin, halves[h]]
            bulk[step, h][3].append(push(place, place, gf_s.at[step, h], gf_r.at[step, h], i, {"grp": partner}))

    def gains_near(step):
        for h in range(HALVES):
            for copy in bulk[step, h][1]:
                copy.wait_recv()

    def gains_last(step):
        for h in range(HALVES):
            for copy in bulk[step, h][3]:
                copy.wait_recv()

    def typed(kinds_row):
        kinds_col = jnp.broadcast_to(kinds_row, (GROUP_LOCAL, n_own)).T[:, :1]
        vectors = jnp.zeros((n_own, units), jnp.float32)
        for kind in range(readout_ref.shape[0]):
            vectors = jnp.where(kinds_col == kind, readout_ref[kind:kind + 1, :], vectors)
        return vectors

    def grouped(member_row):
        return (lax.broadcasted_iota(jnp.int32, (GROUP_LOCAL, n_own), 0).astype(jnp.float32) == member_row).astype(jnp.float32)

    def picked(xs, hot):
        high = xs.astype(jnp.bfloat16).astype(jnp.float32)
        return [(v[:, None, :] * hot[None]).reshape(local * GROUP_LOCAL, n_own).astype(jnp.bfloat16) for v in (high, xs - high)]

    for step in range(STEPS):
        second, third = [], []
        cuts = [pl.ds(0, local + 1)]
        if step == 0:
            hidden = jnp.tanh(triple(atoms_ref[0], current) + bias_ref[...])
            vectors = typed(kinds_ref[:1, :].astype(jnp.float32))
            slope_high, slope_low = split((1.0 - hidden * hidden) * vectors)
            slope_both = jnp.concatenate([slope_high, slope_low], axis=1)
            hot = grouped(member_ref[:1, :].astype(jnp.float32))
            energy = exact(hot, hidden * vectors)
            energy = jnp.broadcast_to(jnp.sum(energy, axis=1, keepdims=True), (GROUP_LOCAL, units))

            def grads(p):
                high, low = picked(xt_ref[pl.ds(p * local, local), :], hot)
                one = jnp.dot(high, slope_both, preferred_element_type=jnp.float32)
                two = jnp.dot(low, slope_high, preferred_element_type=jnp.float32)
                total = one[:, :units] + one[:, units:] + two
                jpart[p, :local] = total.reshape(local, GROUP_LOCAL, units)
                jpart[p, local] = energy

            greet(floor + [{"grp": p} for p in column])
            first = []
            for i, p in enumerate(plane):
                grads(p)
                first.append(push(jpart.at[p], jgot.at[i], j_s, j_r, i, {"atm": p}))
            grads(col)
            total = jpart[col]
            for i, copy in enumerate(first):
                copy.wait_recv()
                total = total + jgot[i]
            jall[step, row] = total
            sends += first
        else:
            def slopes_of(s, energy):
                at = pl.ds(pl.multiple_of(s * n_own, n_own), n_own)
                hidden = jnp.tanh(triple(xa[s], current) + bias_ref[...])
                high, low = split((1.0 - hidden * hidden) * vec[s])
                slopes[at, :] = jnp.concatenate([high, low], axis=1)
                return energy + exact(hots[s], hidden * vec[s])

            energy = lax.fori_loop(0, n_atm, slopes_of, jnp.zeros((GROUP_LOCAL, units), jnp.float32))
            one = jnp.dot(picks[0], slopes[...], preferred_element_type=jnp.float32)
            two = jnp.dot(picks[1], slopes[:, :units], preferred_element_type=jnp.float32)
            total = one[:, :units] + one[:, units:] + two
            jall[step, row, :local] = total.reshape(local, GROUP_LOCAL, units)
            jall[step, row, local] = jnp.broadcast_to(jnp.sum(energy, axis=1, keepdims=True), (GROUP_LOCAL, units))

        place = jall.at[step, row]
        second.append([push(place, place, z_s.at[step], z_r.at[step], i, {"grp": p}) for i, p in enumerate(column)])
        third.append([push(place, place, f_s.at[step], f_r.at[step], len(column), {"grp": partner})])
        sends += second[0]
        if step == 0:
            gather = [push(xa.at[col], xa.at[col], a_s.at[0], a_r.at[0], i, {"atm": p}) for i, p in enumerate(plane)]
            gather += [push(aux.at[col], aux.at[col], a_s.at[1], a_r.at[1], i, {"atm": p}) for i, p in enumerate(plane)]
            sends += gather
            for copy in gather:
                copy.wait_recv()

            def prepare(s, carry):
                at = pl.ds(pl.multiple_of(s * n_own, n_own), n_own)
                hot = grouped(aux[s, 1:2])
                hots[s] = hot
                vec[s] = typed(aux[s, :1])
                xt_ref[...] = xa[s].T
                high, low = picked(xt_ref[pl.ds(col * local, local), :], hot)
                picks[0, :, at] = high
                picks[1, :, at] = low
                return carry
            lax.fori_loop(0, n_atm, prepare, 0)
        else:
            for h in range(HALVES):
                gains_rows(0, h, gpiece[0, halves[h]])
            for copy in early_sends:
                copy.wait_send()

        def forward(k):
            for i, copy in enumerate(second[k]):
                copy.wait_recv()
                origin = lax.rem(z + n_z - (i + 1), n_z) * CORES + core
                place = jall.at[step, origin]
                third[k].append(push(place, place, f_s.at[step], f_r.at[step], i, {"grp": partner}))

        def product(at, over):
            high, low = split(p_ref[pl.ds(at, tall), pl.ds(over, deep)])
            right = both[step, :, pl.ds(over, deep)]
            return across(high, right) + across(low, right)

        def some_rows(k, start, stop):
            def add(t, carry):
                at = pl.multiple_of(t // steps * tall, tall)
                over = pl.multiple_of(k * span + lax.rem(t, steps) * deep, deep)
                tacc[pl.ds(at, tall), :] += product(at, over)
                return carry
            lax.fori_loop(start * steps, stop * steps, add, 0)

        def last_rows(i, carry):
            p = lax.rem(col + 1 + i, n_atm)

            def add(t, carry):
                at = pl.multiple_of(p * piece + t // steps * tall, tall)
                over = pl.multiple_of((PARTS - 1) * span + lax.rem(t, steps) * deep, deep)
                tacc[pl.ds(at, tall), :] += product(at, over)
                return carry
            lax.fori_loop(0, piece // tall * steps, add, 0)
            value = tacc[pl.ds(pl.multiple_of(p * piece, piece), piece), :].T
            tpart[step, p] = value[:groups] + value[groups:]

            @pl.when(i < n_atm - 1)
            def _():
                for h in range(HALVES):
                    spread(h, i).start()
            return carry

        def spread(h, i):
            p = lax.rem(col + 1 + i, n_atm)
            return pltpu.make_async_remote_copy(
                src_ref=tpart.at[step, p, halves[h]], dst_ref=tgot.at[step, i, halves[h]],
                send_sem=t_s.at[step, h, i], recv_sem=t_r.at[step, h, i], device_id={"atm": p}, device_id_type=MESH)

        tacc[...] = jnp.zeros_like(tacc)
        scatter = [[spread(h, i) for i in range(n_atm - 1)] for h in range(HALVES)]
        forward(0)
        if step == 1:
            for h in range(HALVES):
                gains_first(0, h, gpiece[0, halves[h]])
        for k in range(PARTS):
            for copy in third[k]:
                copy.wait_recv()
            sends += third[k]
            for i in range(k * chunk, (k + 1) * chunk):
                high, low = split(jall[step, :, i].reshape(groups, units))
                both[step, :groups, i * units:(i + 1) * units] = high
                both[step, groups:, i * units:(i + 1) * units] = low
            if step == 0:
                loads[k].wait()
            if k < PARTS - 1:
                some_rows(k, 0, rows // tall // 2)
                forward(k + 1)
                some_rows(k, rows // tall // 2, rows // tall)
            else:
                inner = local // CORES
                window = lambda p: pl.ds(core * inner + p * per, per)
                jp_copies = [pltpu.make_async_remote_copy(
                    src_ref=jall.at[step, :, window(p)], dst_ref=jpiece.at[step], send_sem=i_s.at[step, i], recv_sem=i_r.at[step],
                    device_id={"atm": p}, device_id_type=MESH) for i, p in enumerate(plane)]

                @pl.when(col == z)
                def _():
                    for copy in jp_copies:
                        copy.start()
                    jpiece[step] = jall[step, :, window(col)]

                lax.fori_loop(0, n_atm, last_rows, 0)
        for h, half in enumerate(halves):
            sends += scatter[h]
            gain = tpart[step, col, half]
            for i, copy in enumerate(scatter[h]):
                copy.wait_recv()
                gain = gain + tgot[step, i, half]
            gpiece[step, half] = gain
            if step == STEPS - 1:
                gains_first(step, h, gain)
                gains_rows(step, h, gain)
        gain = gpiece[step]

        @pl.when(col != z)
        def _():
            jp_copies[0].wait_recv()

        @pl.when(col == z)
        def _():
            for copy in jp_copies:
                copy.wait_send()

        jp = jnp.concatenate([jpiece[step, :, j].reshape(groups, units) for j in range(per)], axis=1)
        stack = gain if step == 0 else jnp.concatenate([gain] + [gpiece[s] for s in range(step)], axis=0)
        terms = across(jp, stack, precision=precise)
        if step == 0:
            terms = jnp.concatenate([terms[:groups // 2], terms[groups // 2:]], axis=1)
        size = pl.ds(0, terms.shape[0])
        cplane[step, seat, size] = terms
        place = cplane.at[step, seat, size]
        hop = [push(place, place, c_s.at[step], c_r.at[step], i, d) for i, d in enumerate(floor)]
        for copy in hop:
            copy.wait_recv()
        if step == 1:
            for h in range(HALVES):
                gains_second(0, h)
        terms = cplane[step, 0, size]
        for i in range(1, seats):
            terms = terms + cplane[step, i, size]
        cz[step, z, size] = terms
        place = cz.at[step, z, size]
        skip = [push(place, place, d_s.at[step], d_r.at[step], i, {"grp": p}) for i, p in enumerate(column)]
        for copy in skip:
            copy.wait_recv()
        sends += hop + skip
        terms = cz[step, 0, size]
        for i in range(1, n_z):
            terms = terms + cz[step, i, size]
        if step == 0:
            curve = jnp.concatenate([terms[:, :groups], terms[:, groups:]], axis=0)
        else:
            cross = terms[:, groups:]
            early = exact(cross, inverses[0])
            curve = (terms[:, :groups] - across(early, cross, precision=precise)) * (1.0 / forget_rate)
        down = lax.broadcasted_iota(jnp.int32, (groups, groups), 0)
        over = lax.broadcasted_iota(jnp.int32, (groups, groups), 1)
        inverse = 0.5 * (curve + curve.T) + jnp.where(down == over, forget_rate, 0.0)
        inverse = spd_sweep(inverse, 0, groups // 2)
        if step == 1:
            for h in range(HALVES):
                gains_third(0, h)
            gains_second(step, 0)
        inverse = spd_sweep(inverse, groups // 2, groups)
        if step == 1:
            for h in range(1, HALVES):
                gains_second(step, h)
        inverses.append(inverse)
        if step == 1:
            gain = (gain - exact(early, gpiece[0])) * (1.0 / forget_rate)

        predicted = jall[step, :, local].reshape(groups, units).T
        mismatch = jnp.broadcast_to(targets_ref[step:step + 1, :], (GROUP_LOCAL, groups)) - predicted[:GROUP_LOCAL]
        change = triple(exact(mismatch, inverse), gain)
        turn = lax.rem(iota8, per)
        mine = change[:, :units]
        for j in range(1, per):
            mine = jnp.where(turn == j, change[:, j * units:(j + 1) * units], mine)
        wplane[step, seat] = mine
        place = wplane.at[step, seat]
        hop = [push(place, place, w_s.at[step], w_r.at[step], i, d) for i, d in enumerate(floor)]
        if step == 1:
            gains_near(0)
            gains_last(0)
            scaled = inverses[0] * (1.0 / forget_rate ** STEPS)
            for b in range(seats):
                high, low = split(triple(scaled, cols0[b // n_atm, b % n_atm]))
                right_ref[:groups, b * piece:(b + 1) * piece] = high
                right_ref[STEPS * groups:(STEPS + 1) * groups, b * piece:(b + 1) * piece] = low
        for copy in hop:
            copy.wait_recv()
        fold = GROUP_LOCAL // per
        for m in range(seats // fold):
            dense = wplane[step, m * fold]
            for j in range(1, fold):
                dense = jnp.where(iota8 >= j * per, wplane[step, m * fold + j], dense)
            wz[step, z, m * GROUP_LOCAL:(m + 1) * GROUP_LOCAL] = dense
        place = wz.at[step, z]
        skip = [push(place, place, v_s.at[step], v_r.at[step], i, {"grp": p}) for i, p in enumerate(column)]
        sends += hop + skip
        if step == 1:
            past = early * (1.0 / forget_rate)
            for b in range(seats):
                past_c[b] = triple(past, cols0[b // n_atm, b % n_atm])
            for h in range(HALVES):
                gains_third(step, h)
            gains_near(1)
            for p in range(n_atm):
                later = rows1[p] * (1.0 / forget_rate) - triple(past, rows0[p])
                high, low = split(jnp.concatenate([rows0[p], later], axis=0).T)
                left_ref[p * piece:(p + 1) * piece, :] = jnp.concatenate([high, low], axis=1)
        for copy in skip:
            copy.wait_recv()
        current = current + wz[step].reshape(features, units)
        if step == 0:
            early_sends, sends = sends, []

    w_ref[...] = current
    for part in bulk.values():
        sends += sum(part[:3], [])
    for copy in sends:
        copy.wait_send()
    scaled = inverses[1] * (1.0 / forget_rate)

    def last_part(b):
        later = cols1[b // n_atm, lax.rem(b, n_atm)] * (1.0 / forget_rate) - past_c[b]
        high, low = split(triple(scaled, later))
        cut = pl.ds(pl.multiple_of(b * piece, piece), piece)
        right_ref[groups:STEPS * groups, cut] = high
        right_ref[(STEPS + 1) * groups:, cut] = low

    for j in range(n_atm):
        last_part(core * n_atm + j)
    gains_last(1)
    for j in range(n_atm):
        last_part((CORES - 1 - core) * n_atm + j)
    for part in bulk.values():
        for copy in part[3]:
            copy.wait_send()


def fused(*args, n_grp, n_atm):
    atoms, kinds, member, targets, weights, bias, readout, covariance = args
    small = [atoms, kinds, member, targets, weights, bias.reshape(1, -1), readout]
    rows, width = covariance.shape
    units = weights.shape[1]
    groups = GROUP_LOCAL * n_grp
    n_z = n_grp // CORES
    seats = CORES * n_atm
    local = width // units
    piece = rows // n_atm
    per = piece // units
    n_own = atoms.shape[1]
    block = (local + 1, GROUP_LOCAL, units)
    f32 = jnp.float32
    dma = pltpu.SemaphoreType.DMA
    vm = lambda *shape: pltpu.VMEM(shape, f32)
    pair = lambda *shape: [dma((STEPS,) + shape)] * 2
    out_shape = (
        vm(rows, width),
        jax.ShapeDtypeStruct((rows, 2 * STEPS * groups), jnp.bfloat16),
        jax.ShapeDtypeStruct((2 * STEPS * groups, width), jnp.bfloat16),
        jax.ShapeDtypeStruct(weights.shape, f32),
    )
    HBM = pl.BlockSpec(memory_space=pltpu.HBM)
    covar, *outs = pl.pallas_call(
        functools.partial(fused_kernel, n_grp, n_atm),
        out_shape=out_shape,
        in_specs=[HBM] * 8,
        out_specs=(VM,) * len(out_shape),
        scratch_shapes=[pltpu.VMEM(v.shape, v.dtype) for v in small]
        + [vm(n_atm, groups, piece), vm(CORES, n_atm, groups, piece)] * 2
        + [
            vm(seats, groups, piece), vm(n_atm, groups, piece),
            vm(atoms.shape[2], n_own),
            vm(n_atm, n_own, atoms.shape[2]), vm(n_atm, GROUP_LOCAL, n_own), vm(n_atm, n_own, units), vm(n_atm, GROUP_LOCAL, n_own),
            pltpu.VMEM((2, local * GROUP_LOCAL, n_atm * n_own), jnp.bfloat16), pltpu.VMEM((n_atm * n_own, 2 * units), jnp.bfloat16),
            vm(n_atm, *block), vm(n_atm - 1, *block), vm(STEPS, n_grp, *block),
            pltpu.VMEM((STEPS, 2 * groups, width), jnp.bfloat16),
            vm(rows, 2 * groups),
            vm(STEPS, n_atm, groups, piece), vm(STEPS, n_atm - 1, groups, piece),
            vm(STEPS, n_grp, per, GROUP_LOCAL, units), vm(STEPS, groups, piece), vm(STEPS, n_z, groups, piece),
            vm(STEPS, seats, groups, STEPS * groups), vm(STEPS, n_z, groups, STEPS * groups),
            vm(STEPS, seats, GROUP_LOCAL, units), vm(STEPS, n_z, seats * per, units),
            dma((PARTS,)), dma((len(small),)),
        ] + [dma((2, n_atm - 1))] * 2 + [dma((n_atm - 1,))] * 2 + pair(n_z - 1) + pair(n_z)
        + [dma((STEPS, n_atm - 1)), dma((STEPS,))] + pair(HALVES, n_atm - 1)
        + pair(seats - 1) + pair(n_z - 1) + pair(seats - 1) + pair(n_z - 1)
        + pair(HALVES, n_atm - 1) + pair(HALVES, n_z - 1) + pair(HALVES, n_atm - 1) + pair(HALVES, n_atm),
        compiler_params=pltpu.CompilerParams(collective_id=4, has_side_effects=True, vmem_limit_bytes=30 << 20),
        name="updates",
    )(*small, covariance)
    return [pltpu.with_memory_space_constraint(covar, pltpu.VMEM), *outs]


def finish_kernel(tile, p_ref, left_ref, right_ref, w_in, out_ref, w_out, ring, sem):
    w_out[...] = w_in[...]
    rows, width = p_ref.shape
    depth = left_ref.shape[1] // 2
    part = min(width, 512)

    def leave(t):
        slot = lax.rem(t, RING)
        return pltpu.make_async_copy(ring.at[slot], out_ref.at[pl.ds(pl.multiple_of(t * tile, tile), tile)], sem.at[slot])

    def one(t, carry):
        @pl.when(t >= RING)
        def _():
            leave(t - RING).wait()

        here = pl.ds(pl.multiple_of(t * tile, tile), tile)
        slot = lax.rem(t, RING)
        high, low = left_ref[here, :depth], left_ref[here, depth:]
        twice = jnp.concatenate([high, high], axis=1)
        for k in range(0, width, part):
            cut = slice(k, k + part)
            down = jnp.dot(twice, right_ref[:, cut], preferred_element_type=jnp.float32)
            down = down + jnp.dot(low, right_ref[:depth, cut], preferred_element_type=jnp.float32)
            ring[slot, :, cut] = p_ref[here, cut] * (1.0 / forget_rate ** STEPS) - down
        leave(t).start()
        return carry

    lax.fori_loop(0, rows // tile, one, 0)
    for t in range(rows // tile - RING, rows // tile):
        leave(t).wait()


def finish(covar, left, right, weights):
    rows, width = covar.shape
    tile = min(rows // 4, 256)
    return pl.pallas_call(
        functools.partial(finish_kernel, tile),
        out_shape=(jax.ShapeDtypeStruct((rows, width), jnp.float32), jax.ShapeDtypeStruct(weights.shape, jnp.float32)),
        in_specs=[VM] * 4,
        out_specs=(pl.BlockSpec(memory_space=pltpu.HBM), VM),
        scratch_shapes=[pltpu.VMEM((RING, tile, width), jnp.float32), pltpu.SemaphoreType.DMA((RING,))],
        compiler_params=pltpu.CompilerParams(vmem_limit_bytes=30 << 20),
        name="finish",
    )(covar, left, right, weights)


def terms_kernel(groups, jac_ref, p_ref, out_ref, both):
    @pl.when(pl.program_id(0) == 0)
    def _():
        jac = jac_ref[...]
        high = jac.astype(jnp.bfloat16).astype(jnp.float32)
        both[...] = jnp.concatenate([high, jac - high], axis=0).T.astype(jnp.bfloat16)

    high, low = split(p_ref[...])
    one = jnp.dot(high, both[...], preferred_element_type=jnp.float32)
    two = jnp.dot(low, both[...], preferred_element_type=jnp.float32)
    one = one.T
    out_ref[0] = one[:groups] + one[groups:] + two.T[:groups]


def row_terms(covar, jac, n_atm):
    rows, width = covar.shape
    groups = jac.shape[0]
    piece = rows // n_atm
    tile = min(piece, 256)
    per = piece // tile
    return pl.pallas_call(
        functools.partial(terms_kernel, groups),
        grid=(rows // tile,),
        out_shape=jax.ShapeDtypeStruct((n_atm, groups, piece), jnp.float32),
        in_specs=[
            pl.BlockSpec((groups, width), lambda i: (0, 0)),
            pl.BlockSpec((tile, width), lambda i: (i, 0)),
        ],
        out_specs=pl.BlockSpec((1, groups, tile), lambda i: (i // per, 0, lax.rem(i, per))),
        scratch_shapes=[pltpu.VMEM((width, 2 * groups), jnp.bfloat16)],
        compiler_params=pltpu.CompilerParams(vmem_limit_bytes=48 << 20),
        name="row_terms",
    )(jac, covar)


def update_kernel(scale, left_ref, right_ref, p_ref, out_ref, right):
    @pl.when(pl.program_id(0) == 0)
    def _():
        high, low = split(right_ref[...])
        right[...] = jnp.concatenate([high, high, low], axis=0)

    high, low = split(left_ref[...])
    left = jnp.concatenate([high, low, high], axis=1)
    width = p_ref.shape[1]
    part = min(width, 512)
    for k in range(0, width, part):
        down = jnp.dot(left, right[:, k:k + part], preferred_element_type=jnp.float32)
        out_ref[:, k:k + part] = p_ref[:, k:k + part] * scale - down


def final_update(covar, left, right):
    rows, width = covar.shape
    depth = left.shape[1]
    tile = min(rows, 256)
    return pl.pallas_call(
        functools.partial(update_kernel, 1.0 / forget_rate ** STEPS),
        grid=(rows // tile,),
        out_shape=jax.ShapeDtypeStruct((rows, width), jnp.float32),
        in_specs=[
            pl.BlockSpec((tile, depth), lambda i: (i, 0)),
            pl.BlockSpec((depth, width), lambda i: (0, 0)),
            pl.BlockSpec((tile, width), lambda i: (i, 0)),
        ],
        out_specs=pl.BlockSpec((tile, width), lambda i: (i, 0)),
        scratch_shapes=[pltpu.VMEM((3 * depth, width), jnp.bfloat16)],
        compiler_params=pltpu.CompilerParams(vmem_limit_bytes=48 << 20),
        name="final_update",
    )(left, right, covar)


def body(atoms, kinds, member, targets, weights, bias, readout, covariance):
    n_grp, n_atm = lax.axis_size("grp"), lax.axis_size("atm")
    rows, width = covariance.shape
    units = weights.shape[1]
    if n_grp == CORES * n_atm and rows % (n_atm * units) == 0 and GROUP_LOCAL % (rows // (n_atm * units)) == 0:
        return finish(*fused(
            atoms, kinds, member, targets, weights, bias, readout, covariance, n_grp=n_grp, n_atm=n_atm
        ))
    groups = GROUP_LOCAL * n_grp
    dot = functools.partial(jnp.dot, precision=precise)
    current = weights
    past = []
    for step in range(STEPS):
        energies, partial_value = local_terms(
            atoms[step], kinds[step], member[step], current, bias, readout
        )
        blocks = partial_value.reshape(GROUP_LOCAL, n_atm, width).transpose(1, 0, 2)
        tail = jnp.broadcast_to(energies[None, :, None], (n_atm, GROUP_LOCAL, LANES))
        shared = share_grads(jnp.concatenate([blocks, tail], axis=2), n_grp, n_atm)
        shared = shared.reshape(groups, width + LANES)
        jac = shared[:, :width]
        mismatch = targets[step] - shared[:, width]
        terms = row_terms(covariance, jac, n_atm) * (1.0 / forget_rate ** step)
        for age, (rows_old, cols_old, inverse_old) in enumerate(past):
            small = lax.dot_general(jac, cols_old, (((1,), (1,)), ((), ())), precision=precise)
            small = dot(small, inverse_old) * (1.0 / forget_rate ** (step - age))
            terms = terms - jnp.einsum("xy,nyp->nxp", small, rows_old, precision=precise)
        rows, cols = share_gains(terms, n_grp, n_atm)
        part = lax.dot_general(jac, cols, (((1,), (1,)), ((), ())), precision=precise)
        inverse = innovation_inverse(gather_atm(part, n_atm, 2))
        coefficient = dot(inverse, mismatch)
        change = dot(coefficient, cols).reshape(-1, current.shape[1])
        current = current + gather_atm(change, n_atm, 3).reshape(current.shape)
        past.append((rows, cols, inverse))
    left, right = [], []
    for age, (rows, cols, inverse) in enumerate(past):
        scaled = jnp.einsum("nxp,xy->npy", rows, inverse, precision=precise)
        left.append(scaled.reshape(-1, groups) * (1.0 / forget_rate ** (STEPS - age)))
        right.append(cols)
    covar = final_update(covariance, jnp.concatenate(left, axis=1), jnp.concatenate(right, axis=0))
    return (covar, current)


def solution(mesh):
    return jax.shard_map(
        body,
        mesh=mesh,
        in_specs=(
            P(None, ("grp", "atm"), None),
            P(None, ("grp", "atm")),
            P(None, ("grp", "atm")),
            P(),
            P(),
            P(),
            P(),
            P("grp", "atm"),
        ),
        out_specs=(P("grp", "atm"), P()),
        check_vma=False,
    )
```
